256 devices in a mesh: blk: 16 (over x_hi, y, core), rep: 16 (over x_lo, z).
Axes of the slice: x: 4 (x_hi: 2, x_lo: 2; x = x_hi * 2 + x_lo), y: 4, z: 8, core: 2. Of those that a mesh axis runs over, the one named last changes fastest.
Arguments:
- out_grad: bfloat16 [49152, 256], P(('blk', 'rep')), may hold values from -0.59765625 to 0.59765625
- pre_act: bfloat16 [49152, 256], P(('blk', 'rep')), may hold values from -6 to 6
- features: bfloat16 [49152, 256], P(('blk', 'rep')), may hold values from -0.02734375 to 0.02734375
- weight: bfloat16 [256, 256], replicated, may hold values from -0.375 to 0.375
- degrees: int32 [49152], P(('blk', 'rep')), may hold values from 1 to 255
- tiles: bfloat16 [4096, 24, 128, 128], P(('blk', 'rep')), may hold values from 0 to 1, as said below
- tile_rows: int32 [4096, 24], P(('blk', 'rep')), may hold values from 0 to 23, as said below
- tile_cols: int32 [4096, 24], P(('blk', 'rep')), may hold values from 0 to 23, as said below
Outputs:
- input_grad: bfloat16 [49152, 256], P(('blk', 'rep'))
- weight_grad: float32 [256, 256], replicated
The draws below stay inside these ranges and needn't reach their ends.
Inputs may be any that keep to these rules, and one draw needn't show every extreme that they name: `tiles`: entries are 0 or 1. For each device and source row group the slots holding a nonzero tile come first, 1 to 24 of them; all 24 slots are nonzero in at least two source row groups of every device; the other slots are all zero. Within one row group b and one source row group h, the nonzero slots of all 16 devices of b hold distinct (tile_rows, tile_cols) positions; all-zero slots hold 0. `tile_cols`: All-zero slots hold 0.
All inputs are finite; a program needn't handle non-finite values.
Results may differ from the reference program's by a relative error of at most 0.0053.
Values may be sent and summed in bfloat16 or wider, within the bound.
No kernel may reach another device: no remote copies, remote signals or barrier semaphores. Data moves between devices by JAX's collectives and lax.ppermute only.
A program may use at most 128 MiB of HBM per device.

```python
import jax
import jax.numpy as jnp
from jax import lax

F = 256
BS = 128
CYCLE = 16
REPLICAS = 16
GROUP_BLOCKS = 24
CAP = 24
NODES = 49152


def tile_layout(key):
    device_total = CYCLE * REPLICAS
    layout_key = jax.random.fold_in(key, 101)
    key_count, key_favour, key_shuffle = jax.random.split(layout_key, 3)
    counts = jax.random.randint(key_count, (device_total, CYCLE), 1, CAP + 1)
    scores = jax.random.randint(key_favour, (device_total, CYCLE), 0, 1 << 20) * CYCLE + jnp.arange(CYCLE, dtype=jnp.int32)[None, :]
    ranking = jnp.argsort(scores, axis=1)
    group_iota = jnp.arange(CYCLE, dtype=jnp.int32)[None, :]
    full_group = (group_iota == ranking[:, 0:1]) | (group_iota == ranking[:, 1:2])
    counts = jnp.where(full_group, CAP, counts)
    shuffle_keys = jax.random.split(key_shuffle, CYCLE * CYCLE)
    shuffles = jax.vmap(lambda one_key: jax.random.permutation(one_key, GROUP_BLOCKS * GROUP_BLOCKS))(shuffle_keys)
    shuffles = shuffles.reshape(CYCLE, CYCLE, GROUP_BLOCKS * GROUP_BLOCKS)
    device_ids = jnp.arange(device_total, dtype=jnp.int32)
    column_group = device_ids // REPLICAS
    replica = device_ids % REPLICAS
    slot_ids = jnp.arange(CAP, dtype=jnp.int32)
    pick_index = replica[:, None, None] * CAP + slot_ids[None, None, :]
    positions = shuffles[column_group[:, None, None], jnp.arange(CYCLE, dtype=jnp.int32)[None, :, None], pick_index]
    live_slot = slot_ids[None, None, :] < counts[:, :, None]
    row_ids = jnp.where(live_slot, positions // GROUP_BLOCKS, 0)
    col_ids = jnp.where(live_slot, positions % GROUP_BLOCKS, 0)
    return (row_ids.reshape(device_total * CYCLE, CAP).astype(jnp.int32), col_ids.reshape(device_total * CYCLE, CAP).astype(jnp.int32), live_slot.reshape(device_total * CYCLE, CAP))


def draw_tiles(key, part):
    row_ids, col_ids, live_slot = tile_layout(key)
    density = 0.25
    uniform = jax.random.uniform(jax.random.fold_in(key, 202), (CYCLE * REPLICAS * CYCLE, CAP, BS, BS), jnp.float32)
    values = (uniform < density).astype(jnp.float32) * live_slot[:, :, None, None].astype(jnp.float32)
    return values.astype(jnp.bfloat16)


def draw_tile_rows(key, part):
    row_ids, col_ids, live_slot = tile_layout(key)
    return row_ids


def draw_tile_cols(key, part):
    row_ids, col_ids, live_slot = tile_layout(key)
    return col_ids


def draw_degrees(key, part):
    key_power, key_value = jax.random.split(jax.random.fold_in(key, 303))
    powers = jax.random.randint(key_power, (NODES,), 0, 8)
    lower = jnp.left_shift(jnp.ones((NODES,), jnp.int32), powers)
    offsets = jax.random.randint(key_value, (NODES,), 0, 1 << 20) % lower
    return (lower + offsets).astype(jnp.int32)


def block_scale(key, dims, pieces, least, top_value):
    loudness = 1.0
    for dim, shards_of in pieces:
        heights = jax.random.uniform(jax.random.fold_in(jax.random.fold_in(key, 6), dim), (shards_of,), jnp.float32, least / len(pieces), top_value / len(pieces))
        loudness = loudness * jnp.repeat(jnp.exp(heights), dims[dim] // shards_of).reshape((-1,) + (1,) * (len(dims) - 1 - dim))
    return loudness


def centred(stream_key, dims, scale, most, shards=(), kind=jnp.bfloat16):
    values = scale * jax.random.normal(stream_key, dims, jnp.float32)
    if shards:
        values = values * block_scale(stream_key, dims, shards, -0.22, 0.18)
    return jnp.clip(values, -most, most).astype(kind)


def setup_inputs(seed: int = 0) -> dict:
    splits = jax.random.split(jax.random.key(seed), 9)
    out_grad = centred(splits[0], (NODES, F), 0.1, 0.59765625, ((0, 256),))
    pre_act = centred(splits[1], (NODES, F), 1.0, 6.0, ((0, 256),))
    features = centred(splits[2], (NODES, F), NODES ** -0.5, 0.02734375, ((0, 256),))
    weight = centred(splits[3], (F, F), F ** -0.5, 0.375)
    degrees = draw_degrees(jax.random.fold_in(splits[8], 71), 0)
    tiles = draw_tiles(jax.random.fold_in(splits[8], 71), 0)
    tile_rows = draw_tile_rows(jax.random.fold_in(splits[8], 71), 0)
    tile_cols = draw_tile_cols(jax.random.fold_in(splits[8], 71), 0)
    return dict(out_grad=out_grad, pre_act=pre_act, features=features, weight=weight, degrees=degrees, tiles=tiles, tile_rows=tile_rows, tile_cols=tile_cols)


def reference(out_grad, pre_act, features, weight, degrees, tiles, tile_rows, tile_cols):
    inverse_root = lax.rsqrt(degrees.astype(jnp.float32))
    active = (pre_act > 0).astype(jnp.float32)
    scaled = (out_grad.astype(jnp.float32) * active * inverse_root[:, None]).astype(jnp.bfloat16)
    panels = scaled.reshape(CYCLE, GROUP_BLOCKS, BS, F)
    device_total = CYCLE * REPLICAS
    tile_sets = tiles.reshape(device_total, CYCLE, CAP, BS, BS)
    row_sets = tile_rows.reshape(device_total, CYCLE, CAP).astype(jnp.int32)
    col_sets = tile_cols.reshape(device_total, CYCLE, CAP).astype(jnp.int32)
    group_iota = jnp.arange(CYCLE, dtype=jnp.int32)

    def one_device(totals, device):
        column_group = (device // REPLICAS).astype(jnp.int32)
        picked = panels[group_iota[:, None], row_sets[device]]
        products = jnp.einsum('hcji,hcjf->hcif', tile_sets[device].astype(jnp.float32), picked.astype(jnp.float32))
        targets = (column_group * GROUP_BLOCKS + col_sets[device]).reshape(-1).astype(jnp.int32)
        totals = totals.at[targets].add(products.reshape(CYCLE * CAP, BS, F))
        return (totals, None)
    start = jnp.zeros((CYCLE * GROUP_BLOCKS, BS, F), jnp.float32)
    totals, _ = lax.scan(one_device, start, jnp.arange(device_total, dtype=jnp.int32))
    propagated = (inverse_root[:, None] * totals.reshape(NODES, F)).astype(jnp.bfloat16)
    input_grad = jnp.dot(propagated, weight.T, preferred_element_type=jnp.float32).astype(jnp.bfloat16)
    weight_grad = jnp.dot(features.T, propagated, preferred_element_type=jnp.float32)
    return (input_grad, weight_grad)
```

```python
import jax
import jax.numpy as jnp
from jax import lax
from jax.experimental import pallas as pl
from jax.experimental.pallas import tpu as pltpu
from jax.sharding import PartitionSpec as P

NX, NY, NZ, NC = 4, 4, 8, 2
BOTH = ("blk", "rep")
UNROLL = 8


def flat_index(x, y, z, core):
    return (((x // 2) * NY + y) * NC + core) * (2 * NZ) + (x % 2) * NZ + z


def pairs(move):
    result = []
    for x in range(NX):
        for y in range(NY):
            for z in range(NZ):
                for core in range(NC):
                    tx, ty, tz, tc = move(x, y, z, core)
                    result.append((flat_index(x, y, z, core), flat_index(tx % NX, ty % NY, tz % NZ, tc)))
    return result


def along_z(step):
    return pairs(lambda x, y, z, core: (x, y, z + step, core))


def along_q(step):
    return pairs(lambda x, y, z, core: (x + step * core, y + step * (1 - core), z, core))


def along_s(step):
    return pairs(lambda x, y, z, core: (x + step * (1 - core), y + step * core, z, core))


def other_core():
    return pairs(lambda x, y, z, core: (x, y, z, 1 - core))


def send(value, moves):
    return lax.ppermute(value, BOTH, moves)


def ring(value, along, count):
    ahead, behind = along(1), along(-1)
    parts = {0: [value]}
    from_behind, from_ahead = value, value
    for step in range(1, count // 2):
        from_behind = send(from_behind, ahead)
        from_ahead = send(from_ahead, behind)
        parts[count - step] = [from_behind]
        parts[step] = [from_ahead]
    half = value.shape[0] // 2
    parts[count // 2] = [send(from_behind[:half], ahead), send(from_ahead[half:], behind)]
    return [parts[d] for d in range(count)]


def stacked(found):
    return jnp.stack([part[0] if len(part) == 1 else jnp.concatenate(part, axis=0) for part in found])


def products_kernel(chunk_starts, counts, unit0, unit1, columns, core, kept, received, *rest):
    chunks = rest[: len(chunk_starts)]
    own_out, other_out, units, totals, sem = rest[len(chunk_starts):]
    step = pl.program_id(0)

    @pl.when(step == 0)
    def _():
        copies = [
            pltpu.make_async_copy(chunk, units.at[pl.ds(start, chunk.shape[0])], sem.at[n])
            for n, (chunk, start) in enumerate(zip(chunks, chunk_starts))
        ]
        for copy in copies:
            copy.start()
        totals[...] = jnp.zeros_like(totals)
        for copy in copies:
            copy.wait()

    slots = kept.shape[2]
    for side, tiles in ((0, kept), (1, received)):
        base = (side * pl.num_programs(0) + step) * slots

        def batch(i, _):
            found = []
            for k in range(UNROLL):
                slot = i * UNROLL + k
                entry = base + slot
                tile = tiles[0, 0, slot] if side == 0 else tiles[0, slot]
                rows = jnp.concatenate([units[unit0[entry]], units[unit1[entry]]], axis=0)
                found.append((columns[entry], lax.dot_general(
                    tile, rows, (((0,), (0,)), ((), ())), preferred_element_type=jnp.float32)))
            for column, product in found:
                totals[column] += product
            return 0

        live = counts[side * pl.num_programs(0) + step]
        lax.fori_loop(0, (live + UNROLL - 1) // UNROLL, batch, 0)

    @pl.when(step == pl.num_programs(0) - 1)
    def _():
        half = own_out.shape[0]
        own_out[...] = totals[:half]
        other_out[...] = totals[half:].astype(other_out.dtype)


def products(tiles, received, chunks, chunk_starts, counts, unit0, unit1, columns, core):
    groups, _, slots, block, _ = tiles.shape
    width = chunks[0].shape[-1]
    return pl.pallas_call(
        lambda *refs: products_kernel(chunk_starts, *refs),
        out_shape=(
            jax.ShapeDtypeStruct((24, block, width), jnp.float32),
            jax.ShapeDtypeStruct((24, block, width), jnp.bfloat16),
        ),
        grid_spec=pltpu.PrefetchScalarGridSpec(
            num_scalar_prefetch=5,
            grid=(groups,),
            in_specs=[
                pl.BlockSpec((1, 1, slots, block, block), lambda g, n, u, v, k, core: (g, core[0], 0, 0, 0)),
                pl.BlockSpec((1, slots, block, block), lambda g, *_: (g, 0, 0, 0)),
            ] + [pl.BlockSpec(memory_space=pl.ANY)] * len(chunks),
            out_specs=(pl.BlockSpec((24, block, width), lambda g, *_: (0, 0, 0)),) * 2,
            scratch_shapes=[
                pltpu.VMEM((384, 64, width), jnp.bfloat16),
                pltpu.VMEM((48, block, width), jnp.float32),
                pltpu.SemaphoreType.DMA((len(chunks),)),
            ],
        ),
        compiler_params=pltpu.CompilerParams(vmem_limit_bytes=56 << 20),
        cost_estimate=pl.CostEstimate(flops=384 * 2 * block * block * width, bytes_accessed=30 << 20, transcendentals=0),
        name="tile_products",
    )(counts, unit0, unit1, columns, core, tiles, received, *chunks)


def body(out_grad, pre_act, features, weight, degrees, tiles, tile_rows, tile_cols):
    own_blk, own_rep = lax.axis_index("blk"), lax.axis_index("rep")
    core, y = own_blk % NC, (own_blk // NC) % NY
    x = (own_blk // (NC * NY)) * 2 + own_rep // NZ
    z = own_rep % NZ
    width = out_grad.shape[1]
    slots, block = tiles.shape[1], tiles.shape[2]
    groups = tiles.shape[0] // NC

    inverse_root = lax.rsqrt(degrees.astype(jnp.float32))
    active = (pre_act > 0).astype(jnp.float32)
    scaled = (out_grad.astype(jnp.float32) * active * inverse_root[:, None]).astype(jnp.bfloat16)

    odd = own_rep % 2
    full = lax.dynamic_slice_in_dim(scaled, odd * 64, 128, 0)
    half = lax.dynamic_slice_in_dim(scaled, (1 - odd) * 128, 64, 0)

    by_parity = tiles.reshape(groups, NC, slots, block, block)
    flip = other_core()
    passed = lax.dynamic_index_in_dim(by_parity, 1 - core, 1, keepdims=False)
    received = send(passed, flip)
    codes = (tile_rows * 32 + tile_cols).reshape(groups, NC, slots)
    kept_codes = lax.dynamic_index_in_dim(codes, core, 1, keepdims=False)
    received_codes = send(lax.dynamic_index_in_dim(codes, 1 - core, 1, keepdims=False), flip)
    codes = jnp.stack([kept_codes, received_codes])
    rows, cols = codes // 32, codes % 32

    group = jnp.arange(groups)[None, :, None] * NC
    pair, kind = rows // 3, rows % 3
    source_x = (group // (NC * NY)) * 2 + (2 * pair) // NZ
    source_y = (group // NC) % NY
    ahead_x, ahead_y = (source_x - x) % NX, (source_y - y) % NY
    ahead_s = jnp.where(core == 0, ahead_x, ahead_y)
    ahead_q = jnp.where(core == 0, ahead_y, ahead_x)
    first_z, second_z = (2 * pair - z) % NZ, (2 * pair + 1 - z) % NZ
    full_unit = ((ahead_s * 4 + ahead_q) * NZ + jnp.where(kind == 0, first_z, second_z)) * 2
    half_unit = 256 + ahead_q * 4 + ahead_s
    split = kind == 1
    unit0 = jnp.where(split, half_unit + first_z * 16, full_unit).reshape(-1).astype(jnp.int32)
    unit1 = jnp.where(split, half_unit + second_z * 16, full_unit + 1).reshape(-1).astype(jnp.int32)
    columns = (cols + jnp.arange(2)[:, None, None] * 24).reshape(-1).astype(jnp.int32)
    last = jnp.max(jnp.where(codes != 0, jnp.arange(slots) + 1, 0), axis=2)
    counts = jnp.minimum(last + 1, slots).reshape(-1).astype(jnp.int32)

    full_found = ring(stacked(ring(stacked(ring(full, along_z, NZ)), along_q, 4)), along_s, 4)
    half_found = ring(stacked(ring(stacked(ring(half, along_s, 4)), along_q, 4)), along_z, NZ)
    chunks, starts, at = [], [], 0
    for found in (full_found, half_found):
        for part in found:
            for piece in part:
                piece = piece.reshape(-1, 64, width)
                chunks.append(piece)
                starts.append(at)
                at += piece.shape[0]

    own, other = products(
        by_parity, received, chunks, starts, counts, unit0, unit1, columns, core.reshape(1).astype(jnp.int32)
    )
    partial = (own + send(other, flip).astype(jnp.float32)).astype(jnp.bfloat16)
    partial = partial.reshape(-1, width)
    exchanged = lax.all_to_all(partial, "rep", 0, 0, tiled=True)
    summed = exchanged.reshape(2 * NZ, -1, width).astype(jnp.float32).sum(axis=0)

    propagated = (inverse_root[:, None] * summed).astype(jnp.bfloat16)
    input_grad = lax.dot_general(
        propagated, weight, (((1,), (1,)), ((), ())), preferred_element_type=jnp.float32
    ).astype(jnp.bfloat16)
    local_weight = lax.dot_general(
        features, propagated, (((0,), (0,)), ((), ())), preferred_element_type=jnp.float32
    )
    own_rows = lax.all_to_all(local_weight, "rep", 0, 0, tiled=True).reshape(16, 16, width).sum(axis=0)
    spread = jnp.broadcast_to(own_rows[None], (16, 16, width)).reshape(256, width)
    own_rows = lax.all_to_all(spread, "blk", 0, 0, tiled=True).reshape(16, 16, width).sum(axis=0)
    spread = jnp.broadcast_to(own_rows[None], (16, 16, width)).reshape(256, width)
    weight_grad = lax.all_to_all(spread, "rep", 0, 0, tiled=True)
    return (input_grad, weight_grad)


def solution(mesh):
    placed = (
        P(("blk", "rep"), None),
        P(("blk", "rep"), None),
        P(("blk", "rep"), None),
        P(),
        P(("blk", "rep")),
        P(("blk", "rep"), None, None, None),
        P(("blk", "rep"), None),
        P(("blk", "rep"), None),
    )
    return jax.shard_map(
        body, mesh=mesh, in_specs=placed, out_specs=(P(("blk", "rep"), None), P()), check_vma=False
    )
```

```python
import jax
import jax.numpy as jnp
from jax import lax
from jax.experimental import pallas as pl
from jax.experimental.pallas import tpu as pltpu
from jax.sharding import PartitionSpec as P

NX, NY, NZ, NC = 4, 4, 8, 2
BOTH = ("blk", "rep")
UNROLL = 8


def flat_index(x, y, z, core):
    return (((x // 2) * NY + y) * NC + core) * (2 * NZ) + (x % 2) * NZ + z


def pairs(move):
    result = []
    for x in range(NX):
        for y in range(NY):
            for z in range(NZ):
                for core in range(NC):
                    tx, ty, tz, tc = move(x, y, z, core)
                    result.append((flat_index(x, y, z, core), flat_index(tx % NX, ty % NY, tz % NZ, tc)))
    return result


def along_z(step):
    return pairs(lambda x, y, z, core: (x, y, z + step, core))


def along_q(step):
    return pairs(lambda x, y, z, core: (x + step * core, y + step * (1 - core), z, core))


def along_s(step):
    return pairs(lambda x, y, z, core: (x + step * (1 - core), y + step * core, z, core))


def across_x():
    return pairs(lambda x, y, z, core: (x + 1 - 2 * (x % 2), y, z, core))


def other_core():
    return pairs(lambda x, y, z, core: (x, y, z, 1 - core))


def send(value, moves):
    return lax.ppermute(value, BOTH, moves)


def ring_first(value, along):
    return send(value, along(1)), send(value, along(-1))


def ring_last(behind, ahead, along):
    half = behind.shape[0] // 2
    return [send(behind[:half], along(1)), send(ahead[half:], along(-1))]


def together(*values):
    return lax.optimization_barrier(values)


def stacked(found):
    return jnp.stack([part[0] if len(part) == 1 else jnp.concatenate(part, axis=0) for part in found])


def products_kernel(places, counts, unit0, unit1, columns, here, kept, received, *rest):
    chunks = rest[: len(places)]
    own_out, other_out, units, totals, sem = rest[len(places):]
    step = pl.program_id(0)

    @pl.when(step == 0)
    def _():
        copies = [
            pltpu.make_async_copy(chunk.at[pl.ds(0, size)], units.at[pl.ds(start, size)], sem.at[n])
            for n, (chunk, (start, size)) in enumerate(zip(chunks, places))
        ]
        for copy in copies:
            copy.start()
        totals[...] = jnp.zeros_like(totals)
        for copy in copies:
            copy.wait()

    slots = kept.shape[2]
    for side, tiles in ((0, kept), (1, received)):
        base = (side * pl.num_programs(0) + step) * slots

        def batch(i, _):
            found = []
            for k in range(UNROLL):
                slot = i * UNROLL + k
                entry = base + slot
                tile = tiles[0, 0, slot] if side == 0 else tiles[0, slot]
                rows = jnp.concatenate([units[unit0[entry]], units[unit1[entry]]], axis=0)
                found.append((columns[entry], lax.dot_general(
                    tile, rows, (((0,), (0,)), ((), ())), preferred_element_type=jnp.float32)))
            for column, product in found:
                totals[column] += product
            return 0

        live = counts[side * pl.num_programs(0) + step]
        lax.fori_loop(0, (live + UNROLL - 1) // UNROLL, batch, 0)

    @pl.when(step == pl.num_programs(0) - 1)
    def _():
        for rep in range(2 * NZ):
            place = lax.bitwise_xor(rep // NZ, here[1]) * NZ + lax.rem(rep % NZ - here[2] + NZ, NZ)
            for out, side in ((own_out, 0), (other_out, 24)):
                tile = side + 3 * rep // 2
                if rep % 2 == 0:
                    out[place, :128] = totals[tile].astype(out.dtype)
                    out[place, 128:] = totals[tile + 1, :64].astype(out.dtype)
                else:
                    out[place, :64] = totals[tile, 64:].astype(out.dtype)
                    out[place, 64:] = totals[tile + 1].astype(out.dtype)


def combine_kernel(places, own, other, *rest):
    pieces = rest[: len(places)]
    partial, gradient, features, sem = rest[len(places):]
    step = pl.program_id(0)

    @pl.when(step == 0)
    def _():
        copies = [
            pltpu.make_async_copy(piece.at[pl.ds(start, features.shape[1])], features.at[n], sem.at[n])
            for n, (piece, start) in enumerate(zip(pieces, places))
        ]
        for copy in copies:
            copy.start()
        gradient[...] = jnp.zeros_like(gradient)
        for copy in copies:
            copy.wait()

    total = gradient[...]
    for near in range(2):
        rows = (own[near, 0] + other[near, 0].astype(jnp.float32)).astype(partial.dtype)
        partial[near, 0] = rows
        lanes = jnp.concatenate([features[step, 3 * near + n] for n in range(3)], axis=0)
        total += lax.dot_general(lanes, rows, (((0,), (0,)), ((), ())), preferred_element_type=jnp.float32)
    gradient[...] = total


def combine(own, other, pieces, places):
    width = own.shape[-1]
    block = pl.BlockSpec((2, 1, 192, width), lambda d: (0, d, 0, 0))
    return pl.pallas_call(
        lambda *refs: combine_kernel(places, *refs),
        out_shape=(
            jax.ShapeDtypeStruct((2, NZ, 192, width), jnp.bfloat16),
            jax.ShapeDtypeStruct((width, width), jnp.float32),
        ),
        grid_spec=pltpu.PrefetchScalarGridSpec(
            num_scalar_prefetch=0,
            grid=(NZ,),
            in_specs=[block, block] + [pl.BlockSpec(memory_space=pl.ANY)] * NZ,
            out_specs=(block, pl.BlockSpec((width, width), lambda d: (0, 0))),
            scratch_shapes=[pltpu.VMEM((NZ, 6, 64, width), jnp.bfloat16), pltpu.SemaphoreType.DMA((NZ,))],
        ),
        compiler_params=pltpu.CompilerParams(vmem_limit_bytes=56 << 20),
        cost_estimate=pl.CostEstimate(flops=2 * 3072 * width * width, bytes_accessed=8 << 20, transcendentals=0),
        name="combine_cores",
    )(own.reshape(2, NZ, 192, width), other.reshape(2, NZ, 192, width), *pieces)


def pick_kernel(side, tiles, picked, sem):
    copies = [
        pltpu.make_async_copy(tiles.at[group, side[0]], picked.at[group], sem.at[group])
        for group in range(picked.shape[0])
    ]
    for copy in copies:
        copy.start()
    for copy in copies:
        copy.wait()


def pick(tiles, side):
    groups, _, slots, block, _ = tiles.shape
    return pl.pallas_call(
        pick_kernel,
        out_shape=jax.ShapeDtypeStruct((groups, slots, block, block), tiles.dtype),
        grid_spec=pltpu.PrefetchScalarGridSpec(
            num_scalar_prefetch=1,
            grid=(),
            in_specs=[pl.BlockSpec(memory_space=pl.ANY)],
            out_specs=pl.BlockSpec(memory_space=pl.ANY),
            scratch_shapes=[pltpu.SemaphoreType.DMA((groups,))],
        ),
        cost_estimate=pl.CostEstimate(flops=0, bytes_accessed=12 << 20, transcendentals=0),
        name="pick_tiles",
    )(side.reshape(1).astype(jnp.int32), tiles)


def products(tiles, received, chunks, places, counts, unit0, unit1, columns, here):
    groups, _, slots, block, _ = tiles.shape
    width = chunks[0].shape[-1]
    return pl.pallas_call(
        lambda *refs: products_kernel(places, *refs),
        out_shape=(
            jax.ShapeDtypeStruct((2 * NZ, 192, width), jnp.float32),
            jax.ShapeDtypeStruct((2 * NZ, 192, width), jnp.bfloat16),
        ),
        grid_spec=pltpu.PrefetchScalarGridSpec(
            num_scalar_prefetch=5,
            grid=(groups,),
            in_specs=[
                pl.BlockSpec((1, 1, slots, block, block), lambda g, n, u, v, k, here: (g, here[0], 0, 0, 0)),
                pl.BlockSpec((1, slots, block, block), lambda g, *_: (g, 0, 0, 0)),
            ] + [pl.BlockSpec(memory_space=pl.ANY)] * len(chunks),
            out_specs=(pl.BlockSpec((2 * NZ, 192, width), lambda g, *_: (0, 0, 0)),) * 2,
            scratch_shapes=[
                pltpu.VMEM((384, 64, width), jnp.bfloat16),
                pltpu.VMEM((48, block, width), jnp.float32),
                pltpu.SemaphoreType.DMA((len(chunks),)),
            ],
        ),
        compiler_params=pltpu.CompilerParams(vmem_limit_bytes=56 << 20),
        cost_estimate=pl.CostEstimate(flops=384 * 2 * block * block * width, bytes_accessed=30 << 20, transcendentals=0),
        name="tile_products",
    )(counts, unit0, unit1, columns, here, tiles, received, *chunks)


def body(out_grad, pre_act, features, weight, degrees, tiles, tile_rows, tile_cols):
    own_blk, own_rep = lax.axis_index("blk"), lax.axis_index("rep")
    core, y = own_blk % NC, (own_blk // NC) % NY
    x = (own_blk // (NC * NY)) * 2 + own_rep // NZ
    z = own_rep % NZ
    width = out_grad.shape[1]
    slots, block = tiles.shape[1], tiles.shape[2]
    groups = tiles.shape[0] // NC

    inverse_root = lax.rsqrt(degrees.astype(jnp.float32))
    active = (pre_act > 0).astype(jnp.float32)
    scaled = (out_grad.astype(jnp.float32) * active * inverse_root[:, None]).astype(jnp.bfloat16)

    rooted_features = (features.astype(jnp.float32) * inverse_root[:, None]).astype(jnp.bfloat16)

    odd = own_rep % 2
    full = lax.dynamic_slice_in_dim(scaled, odd * 64, 128, 0)
    half = lax.dynamic_slice_in_dim(scaled, (1 - odd) * 128, 64, 0)

    flip = other_core()
    by_parity = tiles.reshape(groups, NC, slots, block, block)
    codes = (tile_rows * 32 + tile_cols).reshape(groups, NC, slots)
    kept_codes = lax.dynamic_index_in_dim(codes, core, 1, keepdims=False)
    received_codes = send(lax.dynamic_index_in_dim(codes, 1 - core, 1, keepdims=False), flip)
    half_s = [half] + [send(half, along_s(-d)) for d in (1, 2, 3)]
    full_z = {1: send(full, along_z(-1)), 7: send(full, along_z(1))}
    far_features = send(rooted_features, across_x())
    *half_s, full, full_z[1], full_z[7], far_features, side = together(
        *half_s, full, full_z[1], full_z[7], far_features, 1 - core)
    picked = pick(by_parity, side)
    half_plane = jnp.stack(half_s)
    half_q = [half_plane] + [send(half_plane, along_q(-d)) for d in (1, 2, 3)]
    far_ahead = send(jnp.stack([full_z[7], full]), along_z(-3))
    far_behind = send(jnp.stack([full_z[7], full, full_z[1]]), along_z(3))
    full_line = jnp.concatenate(
        [jnp.stack([full, full_z[1]]), far_ahead, far_behind, full_z[7][None]])
    half_plane = jnp.concatenate(
        [part for part in half_q] + [rooted_features.reshape(-1, 64, width), far_features.reshape(-1, 64, width)])
    half_plane, full_line, picked = together(half_plane, full_line, picked)
    received = send(picked, flip)
    half_z = {0: [half_plane]}
    behind, ahead = ring_first(half_plane, along_z)
    half_z[7], half_z[1] = [behind], [ahead]
    full_q = {0: [full_line]}
    q_behind, q_ahead = ring_first(full_line, along_q)
    full_q[3], full_q[1], full_q[2] = [q_behind], [q_ahead], ring_last(q_behind, q_ahead, along_q)
    full_plane = stacked([full_q[d] for d in range(4)])
    full_plane, behind, ahead = together(full_plane, behind, ahead)
    full_s = {0: [full_plane]}
    s_behind, s_ahead = ring_first(full_plane, along_s)
    full_s[3], full_s[1], full_s[2] = [s_behind], [s_ahead], ring_last(s_behind, s_ahead, along_s)
    for d in (2, 3):
        behind, ahead = send(behind, along_z(1)), send(ahead, along_z(-1))
        half_z[NZ - d], half_z[d] = [behind], [ahead]
    half_z[4] = ring_last(behind, ahead, along_z)
    full_found = [full_s[d] for d in range(4)]
    half_found = [half_z[d] for d in range(NZ)]

    codes = jnp.stack([kept_codes, received_codes])
    rows, cols = codes // 32, codes % 32

    group = jnp.arange(groups)[None, :, None] * NC
    pair, kind = rows // 3, rows % 3
    source_x = (group // (NC * NY)) * 2 + (2 * pair) // NZ
    source_y = (group // NC) % NY
    ahead_x, ahead_y = (source_x - x) % NX, (source_y - y) % NY
    ahead_s = jnp.where(core == 0, ahead_x, ahead_y)
    ahead_q = jnp.where(core == 0, ahead_y, ahead_x)
    first_z, second_z = (2 * pair - z) % NZ, (2 * pair + 1 - z) % NZ
    full_unit = ((ahead_s * 4 + ahead_q) * NZ + jnp.where(kind == 0, first_z, second_z)) * 2
    half_unit = 256 + ahead_q * 4 + ahead_s
    split = kind == 1
    unit0 = jnp.where(split, half_unit + first_z * 16, full_unit).reshape(-1).astype(jnp.int32)
    unit1 = jnp.where(split, half_unit + second_z * 16, full_unit + 1).reshape(-1).astype(jnp.int32)
    columns = (cols + jnp.arange(2)[:, None, None] * 24).reshape(-1).astype(jnp.int32)
    last = jnp.max(jnp.where(codes != 0, jnp.arange(slots) + 1, 0), axis=2)
    counts = jnp.minimum(last + 1, slots).reshape(-1).astype(jnp.int32)

    chunks, places, at = [], [], 0
    for part in (piece for found in full_found for piece in found):
        chunks.append(part.reshape(-1, 64, width))
        places.append((at, chunks[-1].shape[0]))
        at += chunks[-1].shape[0]
    feature_pieces, feature_places = [], []
    for found in half_found:
        left = 16
        for piece in found:
            count = min(left, piece.shape[0])
            chunks.append(piece)
            places.append((at, count))
            at, left = at + count, left - count
            last_piece, last_count = piece, count
        feature_pieces.append(last_piece)
        feature_places.append(last_count)

    here = jnp.stack([core, own_rep // NZ, z]).astype(jnp.int32)
    own, other = products(by_parity, received, chunks, places, counts, unit0, unit1, columns, here)
    partial, local_weight = combine(own, send(other, flip), feature_pieces, feature_places)
    across = send(partial[1], across_x())
    own_rows = lax.all_to_all(local_weight, "rep", 0, 0, tiled=True).reshape(16, 16, width).sum(axis=0)
    line = (partial[0].astype(jnp.float32) + across.astype(jnp.float32)).astype(jnp.bfloat16)
    own_rows, line = together(own_rows, line)
    terms = [line[0]] + [send(line[d], along_z(d)) for d in range(1, NZ)]
    own_rows, terms[1] = together(own_rows, terms[1])
    spread = jnp.broadcast_to(own_rows[None], (16, 16, width)).reshape(256, width)
    own_rows = lax.all_to_all(spread, "blk", 0, 0, tiled=True).reshape(16, 16, width).sum(axis=0)
    spread = jnp.broadcast_to(own_rows[None], (16, 16, width)).reshape(256, width)
    weight_grad = lax.all_to_all(spread, "rep", 0, 0, tiled=True)

    summed = sum(term.astype(jnp.float32) for term in terms)
    propagated = (inverse_root[:, None] * summed).astype(jnp.bfloat16)
    input_grad = lax.dot_general(
        propagated, weight, (((1,), (1,)), ((), ())), preferred_element_type=jnp.float32
    ).astype(jnp.bfloat16)
    return (input_grad, weight_grad)


def solution(mesh):
    placed = (
        P(("blk", "rep"), None),
        P(("blk", "rep"), None),
        P(("blk", "rep"), None),
        P(),
        P(("blk", "rep")),
        P(("blk", "rep"), None, None, None),
        P(("blk", "rep"), None),
        P(("blk", "rep"), None),
    )
    return jax.shard_map(
        body, mesh=mesh, in_specs=placed, out_specs=(P(("blk", "rep"), None), P()), check_vma=False
    )
```

```python
import jax
import jax.numpy as jnp
from jax import lax
from jax.experimental import pallas as pl
from jax.experimental.pallas import tpu as pltpu
from jax.sharding import PartitionSpec as P

NX, NY, NZ, NC = 4, 4, 8, 2
BOTH = ("blk", "rep")
UNROLL = 8


def flat_index(x, y, z, core):
    return (((x // 2) * NY + y) * NC + core) * (2 * NZ) + (x % 2) * NZ + z


def pairs(move):
    result = []
    for x in range(NX):
        for y in range(NY):
            for z in range(NZ):
                for core in range(NC):
                    tx, ty, tz, tc = move(x, y, z, core)
                    result.append((flat_index(x, y, z, core), flat_index(tx % NX, ty % NY, tz % NZ, tc)))
    return result


def along_z(step):
    return pairs(lambda x, y, z, core: (x, y, z + step, core))


def along_q(step):
    return pairs(lambda x, y, z, core: (x + step * core, y + step * (1 - core), z, core))


def along_s(step):
    return pairs(lambda x, y, z, core: (x + step * (1 - core), y + step * core, z, core))


def spread_over(value, places):
    count = len(places[0])
    copies = jnp.broadcast_to(value[None], (count, *value.shape))
    return lax.all_to_all(copies, BOTH, 0, 0, axis_index_groups=places, tiled=True)


def z_lines():
    return [[flat_index(x, y, z, c) for z in range(NZ)] for x in range(NX) for y in range(NY) for c in range(NC)]


def opposite_x():
    return pairs(lambda x, y, z, core: (x + 2, y, z, core))


def paired_y(bit):
    return pairs(lambda x, y, z, core: (x, y ^ bit, z, core))


def across_x():
    return pairs(lambda x, y, z, core: (x + 1 - 2 * (x % 2), y, z, core))


def other_core():
    return pairs(lambda x, y, z, core: (x, y, z, 1 - core))


def send(value, moves):
    return lax.ppermute(value, BOTH, moves)


def ring_first(value, along):
    return send(value, along(1)), send(value, along(-1))


def ring_last(behind, ahead, along):
    half = behind.shape[0] // 2
    return [send(behind[:half], along(1)), send(ahead[half:], along(-1))]


def together(*values):
    return lax.optimization_barrier(values)


def stacked(found):
    return jnp.stack([part[0] if len(part) == 1 else jnp.concatenate(part, axis=0) for part in found])


def products_kernel(places, counts, unit0, unit1, columns, here, kept, received, *rest):
    chunks = rest[: len(places)]
    own_out, other_out, units, totals, sem = rest[len(places):]
    step = pl.program_id(0)

    @pl.when(step == 0)
    def _():
        copies = [
            pltpu.make_async_copy(chunk.at[pl.ds(0, size)], units.at[pl.ds(start, size)], sem.at[n])
            for n, (chunk, (start, size)) in enumerate(zip(chunks, places))
        ]
        for copy in copies:
            copy.start()
        totals[...] = jnp.zeros_like(totals)
        for copy in copies:
            copy.wait()

    slots = kept.shape[2]
    for side, tiles in ((0, kept), (1, received)):
        base = (side * pl.num_programs(0) + step) * slots

        def batch(i, _):
            found = []
            for k in range(UNROLL):
                slot = i * UNROLL + k
                entry = base + slot
                tile = tiles[0, 0, slot] if side == 0 else tiles[0, slot]
                rows = jnp.concatenate([units[unit0[entry]], units[unit1[entry]]], axis=0)
                found.append((columns[entry], lax.dot_general(
                    tile, rows, (((0,), (0,)), ((), ())), preferred_element_type=jnp.float32)))
            for column, product in found:
                totals[column] += product
            return 0

        live = counts[side * pl.num_programs(0) + step]
        lax.fori_loop(0, (live + UNROLL - 1) // UNROLL, batch, 0)

    @pl.when(step == pl.num_programs(0) - 1)
    def _():
        half = own_out.shape[0]
        own_out[...] = totals[:half]
        other_out[...] = totals[half:].astype(other_out.dtype)


def combine_kernel(places, here, own, other, *rest):
    pieces = rest[: len(places)]
    partial, gradient, features, sem = rest[len(places):]
    step = pl.program_id(0)

    @pl.when(step == 0)
    def _():
        copies = [
            pltpu.make_async_copy(piece.at[pl.ds(start, features.shape[1])], features.at[n], sem.at[n])
            for n, (piece, start) in enumerate(zip(pieces, places))
        ]
        for copy in copies:
            copy.start()
        gradient[...] = jnp.zeros_like(gradient)
        for copy in copies:
            copy.wait()

    total = gradient[...]
    ahead = lax.rem(step - here[2] + NZ, NZ)
    for low in range(2):
        rows = (own[low, 0] + other[low, 0].astype(jnp.float32)).astype(partial.dtype)
        partial[low, 0] = rows
        near = lax.bitwise_xor(low, here[1])
        lanes = jnp.concatenate([features[ahead, 3 * near + n] for n in range(3)], axis=0)
        total += lax.dot_general(lanes, rows, (((0,), (0,)), ((), ())), preferred_element_type=jnp.float32)
    gradient[...] = total


def combine(own, other, pieces, places, here):
    width = own.shape[-1]
    block = pl.BlockSpec((2, 1, 192, width), lambda d, here: (0, d, 0, 0))
    return pl.pallas_call(
        lambda *refs: combine_kernel(places, *refs),
        out_shape=(
            jax.ShapeDtypeStruct((2, NZ, 192, width), jnp.bfloat16),
            jax.ShapeDtypeStruct((width, width), jnp.float32),
        ),
        grid_spec=pltpu.PrefetchScalarGridSpec(
            num_scalar_prefetch=1,
            grid=(NZ,),
            in_specs=[block, block] + [pl.BlockSpec(memory_space=pl.ANY)] * NZ,
            out_specs=(block, pl.BlockSpec((width, width), lambda d, here: (0, 0))),
            scratch_shapes=[pltpu.VMEM((NZ, 6, 64, width), jnp.bfloat16), pltpu.SemaphoreType.DMA((NZ,))],
        ),
        compiler_params=pltpu.CompilerParams(vmem_limit_bytes=56 << 20),
        cost_estimate=pl.CostEstimate(flops=2 * 3072 * width * width, bytes_accessed=8 << 20, transcendentals=0),
        name="combine_cores",
    )(here, own.reshape(2, NZ, 192, width), other.reshape(2, NZ, 192, width), *pieces)


def pick_kernel(side, tiles, picked):
    picked[...] = tiles[:, 0]


def pick(tiles, side):
    groups, _, slots, block, _ = tiles.shape
    return pl.pallas_call(
        pick_kernel,
        out_shape=jax.ShapeDtypeStruct((groups, slots, block, block), tiles.dtype),
        grid_spec=pltpu.PrefetchScalarGridSpec(
            num_scalar_prefetch=1,
            grid=(groups,),
            in_specs=[pl.BlockSpec((1, 1, slots, block, block), lambda g, side: (g, side[0], 0, 0, 0))],
            out_specs=pl.BlockSpec((1, slots, block, block), lambda g, side: (g, 0, 0, 0)),
        ),
        cost_estimate=pl.CostEstimate(flops=0, bytes_accessed=12 << 20, transcendentals=0),
        name="pick_tiles",
    )(side.reshape(1).astype(jnp.int32), tiles)


def products(tiles, received, chunks, places, counts, unit0, unit1, columns, here):
    groups, _, slots, block, _ = tiles.shape
    width = chunks[0].shape[-1]
    return pl.pallas_call(
        lambda *refs: products_kernel(places, *refs),
        out_shape=(
            jax.ShapeDtypeStruct((24, block, width), jnp.float32),
            jax.ShapeDtypeStruct((24, block, width), jnp.bfloat16),
        ),
        grid_spec=pltpu.PrefetchScalarGridSpec(
            num_scalar_prefetch=5,
            grid=(groups,),
            in_specs=[
                pl.BlockSpec((1, 1, slots, block, block), lambda g, n, u, v, k, here: (g, here[0], 0, 0, 0)),
                pl.BlockSpec((1, slots, block, block), lambda g, *_: (g, 0, 0, 0)),
            ] + [pl.BlockSpec(memory_space=pl.ANY)] * len(chunks),
            out_specs=(pl.BlockSpec((24, block, width), lambda g, *_: (0, 0, 0)),) * 2,
            scratch_shapes=[
                pltpu.VMEM((384, 64, width), jnp.bfloat16),
                pltpu.VMEM((48, block, width), jnp.float32),
                pltpu.SemaphoreType.DMA((len(chunks),)),
            ],
        ),
        compiler_params=pltpu.CompilerParams(vmem_limit_bytes=56 << 20),
        cost_estimate=pl.CostEstimate(flops=384 * 2 * block * block * width, bytes_accessed=30 << 20, transcendentals=0),
        name="tile_products",
    )(counts, unit0, unit1, columns, here, tiles, received, *chunks)


def body(out_grad, pre_act, features, weight, degrees, tiles, tile_rows, tile_cols):
    own_blk, own_rep = lax.axis_index("blk"), lax.axis_index("rep")
    core, y = own_blk % NC, (own_blk // NC) % NY
    x = (own_blk // (NC * NY)) * 2 + own_rep // NZ
    z = own_rep % NZ
    width = out_grad.shape[1]
    slots, block = tiles.shape[1], tiles.shape[2]
    groups = tiles.shape[0] // NC

    inverse_root = lax.rsqrt(degrees.astype(jnp.float32))
    active = (pre_act > 0).astype(jnp.float32)
    scaled = (out_grad.astype(jnp.float32) * active * inverse_root[:, None]).astype(jnp.bfloat16)

    rooted_features = (features.astype(jnp.float32) * inverse_root[:, None]).astype(jnp.bfloat16)

    odd = own_rep % 2
    full = lax.dynamic_slice_in_dim(scaled, odd * 64, 128, 0)
    half = lax.dynamic_slice_in_dim(scaled, (1 - odd) * 128, 64, 0)

    flip = other_core()
    by_parity = tiles.reshape(groups, NC, slots, block, block)
    codes = (tile_rows * 32 + tile_cols).reshape(groups, NC, slots)
    kept_codes = lax.dynamic_index_in_dim(codes, core, 1, keepdims=False)
    received_codes = send(lax.dynamic_index_in_dim(codes, 1 - core, 1, keepdims=False), flip)
    far_features = send(rooted_features, across_x())
    full_line = spread_over(full, z_lines())
    half_line = jnp.stack([half] + [send(half, along_s(-d)) for d in (1, 2, 3)])
    half_q = [half_line] + [send(half_line, along_q(-d)) for d in (1, 2, 3)]
    picked = pick(by_parity, 1 - core)
    half_plane = jnp.concatenate(
        half_q + [rooted_features.reshape(-1, 64, width), far_features.reshape(-1, 64, width)])
    half_plane, full_line, picked = together(half_plane, full_line, picked)
    received = send(picked, flip)
    half_z = {0: [half_plane]}
    behind, ahead = ring_first(half_plane, along_z)
    half_z[7], half_z[1] = [behind], [ahead]
    full_q = {0: [full_line]}
    q_behind, q_ahead = ring_first(full_line, along_q)
    full_q[3], full_q[1], full_q[2] = [q_behind], [q_ahead], ring_last(q_behind, q_ahead, along_q)
    full_plane = stacked([full_q[d] for d in range(4)])
    full_plane, behind, ahead = together(full_plane, behind, ahead)
    full_s = {0: [full_plane]}
    s_behind, s_ahead = ring_first(full_plane, along_s)
    full_s[3], full_s[1], full_s[2] = [s_behind], [s_ahead], ring_last(s_behind, s_ahead, along_s)
    for d in (2, 3):
        behind, ahead = send(behind, along_z(1)), send(ahead, along_z(-1))
        half_z[NZ - d], half_z[d] = [behind], [ahead]
    half_z[4] = ring_last(behind, ahead, along_z)
    full_found = [full_s[d] for d in range(4)]
    half_found = [half_z[d] for d in range(NZ)]

    codes = jnp.stack([kept_codes, received_codes])
    rows, cols = codes // 32, codes % 32

    group = jnp.arange(groups)[None, :, None] * NC
    pair, kind = rows // 3, rows % 3
    source_x = (group // (NC * NY)) * 2 + (2 * pair) // NZ
    source_y = (group // NC) % NY
    ahead_x, ahead_y = (source_x - x) % NX, (source_y - y) % NY
    ahead_s = jnp.where(core == 0, ahead_x, ahead_y)
    ahead_q = jnp.where(core == 0, ahead_y, ahead_x)
    first_z, second_z = (2 * pair - z) % NZ, (2 * pair + 1 - z) % NZ
    full_unit = ((ahead_s * 4 + ahead_q) * NZ + (2 * pair + kind // 2) % NZ) * 2
    half_unit = 256 + ahead_q * 4 + ahead_s
    split = kind == 1
    unit0 = jnp.where(split, half_unit + first_z * 16, full_unit).reshape(-1).astype(jnp.int32)
    unit1 = jnp.where(split, half_unit + second_z * 16, full_unit + 1).reshape(-1).astype(jnp.int32)
    columns = (cols + jnp.arange(2)[:, None, None] * 24).reshape(-1).astype(jnp.int32)
    last = jnp.max(jnp.where(codes != 0, jnp.arange(slots) + 1, 0), axis=2)
    counts = jnp.minimum(last + 1, slots).reshape(-1).astype(jnp.int32)

    chunks, places, at = [], [], 0
    for part in (piece for found in full_found for piece in found):
        chunks.append(part.reshape(-1, 64, width))
        places.append((at, chunks[-1].shape[0]))
        at += chunks[-1].shape[0]
    feature_pieces, feature_places = [], []
    for found in half_found:
        left = 16
        for piece in found:
            count = min(left, piece.shape[0])
            chunks.append(piece)
            places.append((at, count))
            at, left = at + count, left - count
            last_piece, last_count = piece, count
        feature_pieces.append(last_piece)
        feature_places.append(last_count)

    here = jnp.stack([core, own_rep // NZ, z]).astype(jnp.int32)
    own, other = products(by_parity, received, chunks, places, counts, unit0, unit1, columns, here)
    partial, local_weight = combine(own, send(other, flip), feature_pieces, feature_places, here)
    near = lax.dynamic_index_in_dim(partial, own_rep // NZ, 0, keepdims=False)
    across = send(lax.dynamic_index_in_dim(partial, 1 - own_rep // NZ, 0, keepdims=False), across_x())
    own_rows = lax.all_to_all(local_weight, "rep", 0, 0, tiled=True).reshape(16, 16, width).sum(axis=0)
    line = (near.astype(jnp.float32) + across.astype(jnp.float32)).astype(jnp.bfloat16)
    line, own_rows = together(line, own_rows)
    terms = lax.all_to_all(line, BOTH, 0, 0, axis_index_groups=z_lines(), tiled=True)
    for partner in (other_core(), opposite_x(), paired_y(1), paired_y(2)):
        own_rows = own_rows + send(own_rows, partner)
    own_rows, terms = together(own_rows, terms)
    spread = jnp.broadcast_to(own_rows[None], (16, 16, width)).reshape(256, width)
    weight_grad = lax.all_to_all(spread, "rep", 0, 0, tiled=True)
    summed = terms.astype(jnp.float32).sum(axis=0)

    propagated = (inverse_root[:, None] * summed).astype(jnp.bfloat16)
    input_grad = lax.dot_general(
        propagated, weight, (((1,), (1,)), ((), ())), preferred_element_type=jnp.float32
    ).astype(jnp.bfloat16)
    return (input_grad, weight_grad)


def solution(mesh):
    placed = (
        P(("blk", "rep"), None),
        P(("blk", "rep"), None),
        P(("blk", "rep"), None),
        P(),
        P(("blk", "rep")),
        P(("blk", "rep"), None, None, None),
        P(("blk", "rep"), None),
        P(("blk", "rep"), None),
    )
    return jax.shard_map(
        body, mesh=mesh, in_specs=placed, out_specs=(P(("blk", "rep"), None), P()), check_vma=False
    )
```

```python
import jax
import jax.numpy as jnp
from jax import lax
from jax.experimental import pallas as pl
from jax.experimental.pallas import tpu as pltpu
from jax.sharding import PartitionSpec as P

NX, NY, NZ, NC = 4, 4, 8, 2
BOTH = ("blk", "rep")
UNROLL = 8


def flat_index(x, y, z, core):
    return (((x // 2) * NY + y) * NC + core) * (2 * NZ) + (x % 2) * NZ + z


def pairs(move):
    result = []
    for x in range(NX):
        for y in range(NY):
            for z in range(NZ):
                for core in range(NC):
                    tx, ty, tz, tc = move(x, y, z, core)
                    result.append((flat_index(x, y, z, core), flat_index(tx % NX, ty % NY, tz % NZ, tc)))
    return result


def along_z(step):
    return pairs(lambda x, y, z, core: (x, y, z + step, core))


def along_q(step):
    return pairs(lambda x, y, z, core: (x + step * core, y + step * (1 - core), z, core))


def along_s(step):
    return pairs(lambda x, y, z, core: (x + step * (1 - core), y + step * core, z, core))


def spread_over(value, places):
    count = len(places[0])
    copies = jnp.broadcast_to(value[None], (count, *value.shape))
    return lax.all_to_all(copies, BOTH, 0, 0, axis_index_groups=places, tiled=True)


def z_lines():
    return [[flat_index(x, y, z, c) for z in range(NZ)] for x in range(NX) for y in range(NY) for c in range(NC)]


def opposite_x():
    return pairs(lambda x, y, z, core: (x + 2, y, z, core))


def paired_y(bit):
    return pairs(lambda x, y, z, core: (x, y ^ bit, z, core))


def across_x():
    return pairs(lambda x, y, z, core: (x + 1 - 2 * (x % 2), y, z, core))


def other_core():
    return pairs(lambda x, y, z, core: (x, y, z, 1 - core))


def send(value, moves):
    return lax.ppermute(value, BOTH, moves)


def ring_first(value, along):
    return send(value, along(1)), send(value, along(-1))


def ring_last(behind, ahead, along):
    half = behind.shape[0] // 2
    return [send(behind[:half], along(1)), send(ahead[half:], along(-1))]


def together(*values):
    return lax.optimization_barrier(values)


def stacked(found):
    return jnp.stack([part[0] if len(part) == 1 else jnp.concatenate(part, axis=0) for part in found])


def products_kernel(places, counts, unit0, unit1, columns, here, kept, received, *rest):
    chunks = rest[: len(places)]
    own_out, other_out, units, totals, sem = rest[len(places):]
    step = pl.program_id(0)

    @pl.when(step == 0)
    def _():
        copies = [
            pltpu.make_async_copy(chunk.at[pl.ds(0, size)], units.at[pl.ds(start, size)], sem.at[n])
            for n, (chunk, (start, size)) in enumerate(zip(chunks, places))
        ]
        for copy in copies:
            copy.start()
        totals[...] = jnp.zeros_like(totals)
        for copy in copies:
            copy.wait()

    slots = kept.shape[2]
    for side, tiles in ((0, kept), (1, received)):
        base = (side * pl.num_programs(0) + step) * slots

        def batch(i, _):
            found = []
            for k in range(UNROLL):
                slot = i * UNROLL + k
                entry = base + slot
                tile = tiles[0, 0, slot] if side == 0 else tiles[0, slot]
                rows = jnp.concatenate([units[unit0[entry]], units[unit1[entry]]], axis=0)
                found.append((columns[entry], lax.dot_general(
                    tile, rows, (((0,), (0,)), ((), ())), preferred_element_type=jnp.float32)))
            for column, product in found:
                totals[column] += product
            return 0

        live = counts[side * pl.num_programs(0) + step]
        lax.fori_loop(0, (live + UNROLL - 1) // UNROLL, batch, 0)

    @pl.when(step == pl.num_programs(0) - 1)
    def _():
        half = own_out.shape[0]
        own_out[...] = totals[:half]
        other_out[...] = totals[half:].astype(other_out.dtype)


def features_kernel(places, here, partial, *rest):
    pieces = rest[: len(places)]
    gradient, features, sem = rest[len(places):]
    step = pl.program_id(0)

    @pl.when(step == 0)
    def _():
        copies = [
            pltpu.make_async_copy(piece.at[pl.ds(start, features.shape[1])], features.at[n], sem.at[n])
            for n, (piece, start) in enumerate(zip(pieces, places))
        ]
        for copy in copies:
            copy.start()
        gradient[...] = jnp.zeros_like(gradient)
        for copy in copies:
            copy.wait()

    total = gradient[...]
    for part in range(2):
        place = 2 * step + part
        ahead = lax.rem(place - here[2] + NZ, NZ)
        for low in range(2):
            near = lax.bitwise_xor(low, here[1])
            lanes = jnp.concatenate([features[ahead, 3 * near + n] for n in range(3)], axis=0)
            total += lax.dot_general(
                lanes, partial[low, part], (((0,), (0,)), ((), ())), preferred_element_type=jnp.float32)
    gradient[...] = total


def features_product(partial, pieces, places, here):
    width = partial.shape[-1]
    return pl.pallas_call(
        lambda *refs: features_kernel(places, *refs),
        out_shape=jax.ShapeDtypeStruct((width, width), jnp.float32),
        grid_spec=pltpu.PrefetchScalarGridSpec(
            num_scalar_prefetch=1,
            grid=(NZ // 2,),
            in_specs=[pl.BlockSpec((2, 2, 192, width), lambda d, here: (0, d, 0, 0))]
            + [pl.BlockSpec(memory_space=pl.ANY)] * NZ,
            out_specs=pl.BlockSpec((width, width), lambda d, here: (0, 0)),
            scratch_shapes=[pltpu.VMEM((NZ, 6, 64, width), jnp.bfloat16), pltpu.SemaphoreType.DMA((NZ,))],
        ),
        compiler_params=pltpu.CompilerParams(vmem_limit_bytes=56 << 20),
        cost_estimate=pl.CostEstimate(flops=2 * 3072 * width * width, bytes_accessed=4 << 20, transcendentals=0),
        name="features_product",
    )(here, partial, *pieces)


def pick_kernel(side, tiles, picked, held, in_sem, out_sem):
    groups = range(picked.shape[0])
    reads = [pltpu.make_async_copy(tiles.at[g, side[0]], held.at[g], in_sem.at[g]) for g in groups]
    writes = [pltpu.make_async_copy(held.at[g], picked.at[g], out_sem.at[g]) for g in groups]
    for read in reads:
        read.start()
    for read, write in zip(reads, writes):
        read.wait()
        write.start()
    for write in writes:
        write.wait()


def pick(tiles, side):
    groups, _, slots, block, _ = tiles.shape
    return pl.pallas_call(
        pick_kernel,
        out_shape=jax.ShapeDtypeStruct((groups, slots, block, block), tiles.dtype),
        grid_spec=pltpu.PrefetchScalarGridSpec(
            num_scalar_prefetch=1,
            grid=(),
            in_specs=[pl.BlockSpec(memory_space=pl.ANY)],
            out_specs=pl.BlockSpec(memory_space=pl.ANY),
            scratch_shapes=[
                pltpu.VMEM((groups, slots, block, block), tiles.dtype),
                pltpu.SemaphoreType.DMA((groups,)),
                pltpu.SemaphoreType.DMA((groups,)),
            ],
        ),
        compiler_params=pltpu.CompilerParams(vmem_limit_bytes=16 << 20),
        cost_estimate=pl.CostEstimate(flops=0, bytes_accessed=12 << 20, transcendentals=0),
        name="pick_tiles",
    )(side.reshape(1).astype(jnp.int32), tiles)


def products(tiles, received, chunks, places, counts, unit0, unit1, columns, here):
    groups, _, slots, block, _ = tiles.shape
    width = chunks[0].shape[-1]
    return pl.pallas_call(
        lambda *refs: products_kernel(places, *refs),
        out_shape=(
            jax.ShapeDtypeStruct((24, block, width), jnp.float32),
            jax.ShapeDtypeStruct((24, block, width), jnp.bfloat16),
        ),
        grid_spec=pltpu.PrefetchScalarGridSpec(
            num_scalar_prefetch=5,
            grid=(groups,),
            in_specs=[
                pl.BlockSpec((1, 1, slots, block, block), lambda g, n, u, v, k, here: (g, here[0], 0, 0, 0)),
                pl.BlockSpec((1, slots, block, block), lambda g, *_: (g, 0, 0, 0)),
            ] + [pl.BlockSpec(memory_space=pl.ANY)] * len(chunks),
            out_specs=(pl.BlockSpec((24, block, width), lambda g, *_: (0, 0, 0)),) * 2,
            scratch_shapes=[
                pltpu.VMEM((384, 64, width), jnp.bfloat16),
                pltpu.VMEM((48, block, width), jnp.float32),
                pltpu.SemaphoreType.DMA((len(chunks),)),
            ],
        ),
        compiler_params=pltpu.CompilerParams(vmem_limit_bytes=56 << 20),
        cost_estimate=pl.CostEstimate(flops=384 * 2 * block * block * width, bytes_accessed=30 << 20, transcendentals=0),
        name="tile_products",
    )(counts, unit0, unit1, columns, here, tiles, received, *chunks)


def body(out_grad, pre_act, features, weight, degrees, tiles, tile_rows, tile_cols):
    own_blk, own_rep = lax.axis_index("blk"), lax.axis_index("rep")
    core, y = own_blk % NC, (own_blk // NC) % NY
    x = (own_blk // (NC * NY)) * 2 + own_rep // NZ
    z = own_rep % NZ
    width = out_grad.shape[1]
    slots, block = tiles.shape[1], tiles.shape[2]
    groups = tiles.shape[0] // NC

    inverse_root = lax.rsqrt(degrees.astype(jnp.float32))
    active = (pre_act > 0).astype(jnp.float32)
    scaled = (out_grad.astype(jnp.float32) * active * inverse_root[:, None]).astype(jnp.bfloat16)

    rooted_features = (features.astype(jnp.float32) * inverse_root[:, None]).astype(jnp.bfloat16)

    odd = own_rep % 2
    full = lax.dynamic_slice_in_dim(scaled, odd * 64, 128, 0)
    half = lax.dynamic_slice_in_dim(scaled, (1 - odd) * 128, 64, 0)

    flip = other_core()
    by_parity = tiles.reshape(groups, NC, slots, block, block)
    codes = (tile_rows * 32 + tile_cols).reshape(groups, NC, slots)
    kept_codes = lax.dynamic_index_in_dim(codes, core, 1, keepdims=False)
    received_codes = send(lax.dynamic_index_in_dim(codes, 1 - core, 1, keepdims=False), flip)
    far_features = send(rooted_features, across_x())
    full_line = spread_over(full, z_lines())
    half_line = jnp.stack([half] + [send(half, along_s(-d)) for d in (1, 2, 3)])
    half_q = [half_line] + [send(half_line, along_q(-d)) for d in (1, 2, 3)]
    half_plane = jnp.concatenate(
        half_q + [rooted_features.reshape(-1, 64, width), far_features.reshape(-1, 64, width)])
    half_plane, full_line = together(half_plane, full_line)
    half_z = {0: [half_plane]}
    behind, ahead = ring_first(half_plane, along_z)
    half_z[7], half_z[1] = [behind], [ahead]
    full_q = {0: [full_line]}
    q_behind, q_ahead = ring_first(full_line, along_q)
    full_q[3], full_q[1], full_q[2] = [q_behind], [q_ahead], ring_last(q_behind, q_ahead, along_q)
    full_plane = stacked([full_q[d] for d in range(4)])
    full_plane, behind, ahead, side = together(full_plane, behind, ahead, 1 - core)
    first, second = full_plane[:2], full_plane[2:]
    first_behind, second_ahead = send(first, along_s(1)), send(second, along_s(-1))
    second_behind, first_ahead = send(second, along_s(1)), send(first, along_s(-1))
    full_s = [[first, second], [first_ahead, second_ahead],
              [send(first_behind, along_s(1)), send(second_ahead, along_s(-1))], [first_behind, second_behind]]
    received = send(pick(by_parity, side), flip)
    for d in (2, 3):
        behind, ahead = send(behind, along_z(1)), send(ahead, along_z(-1))
        half_z[NZ - d], half_z[d] = [behind], [ahead]
    half_z[4] = ring_last(behind, ahead, along_z)
    full_found = full_s
    half_found = [half_z[d] for d in range(NZ)]

    codes = jnp.stack([kept_codes, received_codes])
    rows, cols = codes // 32, codes % 32

    group = jnp.arange(groups)[None, :, None] * NC
    pair, kind = rows // 3, rows % 3
    source_x = (group // (NC * NY)) * 2 + (2 * pair) // NZ
    source_y = (group // NC) % NY
    ahead_x, ahead_y = (source_x - x) % NX, (source_y - y) % NY
    ahead_s = jnp.where(core == 0, ahead_x, ahead_y)
    ahead_q = jnp.where(core == 0, ahead_y, ahead_x)
    first_z, second_z = (2 * pair - z) % NZ, (2 * pair + 1 - z) % NZ
    full_unit = ((ahead_s * 4 + ahead_q) * NZ + (2 * pair + kind // 2) % NZ) * 2
    half_unit = 256 + ahead_q * 4 + ahead_s
    split = kind == 1
    unit0 = jnp.where(split, half_unit + first_z * 16, full_unit).reshape(-1).astype(jnp.int32)
    unit1 = jnp.where(split, half_unit + second_z * 16, full_unit + 1).reshape(-1).astype(jnp.int32)
    columns = (cols + jnp.arange(2)[:, None, None] * 24).reshape(-1).astype(jnp.int32)
    last = jnp.max(jnp.where(codes != 0, jnp.arange(slots) + 1, 0), axis=2)
    counts = jnp.minimum(last + 1, slots).reshape(-1).astype(jnp.int32)

    chunks, places, at = [], [], 0
    for part in (piece for found in full_found for piece in found):
        chunks.append(part.reshape(-1, 64, width))
        places.append((at, chunks[-1].shape[0]))
        at += chunks[-1].shape[0]
    feature_pieces, feature_places = [], []
    for found in half_found:
        left = 16
        for piece in found:
            count = min(left, piece.shape[0])
            chunks.append(piece)
            places.append((at, count))
            at, left = at + count, left - count
            last_piece, last_count = piece, count
        feature_pieces.append(last_piece)
        feature_places.append(last_count)

    here = jnp.stack([core, own_rep // NZ, z]).astype(jnp.int32)
    own, other = products(by_parity, received, chunks, places, counts, unit0, unit1, columns, here)
    partial = (own + send(other, flip).astype(jnp.float32)).astype(jnp.bfloat16).reshape(2, NZ, -1, width)
    local_weight = features_product(partial, feature_pieces, feature_places, here)
    near = lax.dynamic_index_in_dim(partial, own_rep // NZ, 0, keepdims=False)
    across = send(lax.dynamic_index_in_dim(partial, 1 - own_rep // NZ, 0, keepdims=False), across_x())
    own_rows = lax.all_to_all(local_weight, "rep", 0, 0, tiled=True).reshape(16, 16, width).sum(axis=0)
    line = (near.astype(jnp.float32) + across.astype(jnp.float32)).astype(jnp.bfloat16)
    line, own_rows = together(line, own_rows)
    terms = lax.all_to_all(line, BOTH, 0, 0, axis_index_groups=z_lines(), tiled=True)
    for partner in (other_core(), opposite_x(), paired_y(1), paired_y(2)):
        own_rows = own_rows + send(own_rows, partner)
    own_rows, terms = together(own_rows, terms)
    spread = jnp.broadcast_to(own_rows[None], (16, 16, width)).reshape(256, width)
    weight_grad = lax.all_to_all(spread, "rep", 0, 0, tiled=True)
    summed = terms.astype(jnp.float32).sum(axis=0)

    propagated = (inverse_root[:, None] * summed).astype(jnp.bfloat16)
    input_grad = lax.dot_general(
        propagated, weight, (((1,), (1,)), ((), ())), preferred_element_type=jnp.float32
    ).astype(jnp.bfloat16)
    return (input_grad, weight_grad)


def solution(mesh):
    placed = (
        P(("blk", "rep"), None),
        P(("blk", "rep"), None),
        P(("blk", "rep"), None),
        P(),
        P(("blk", "rep")),
        P(("blk", "rep"), None, None, None),
        P(("blk", "rep"), None),
        P(("blk", "rep"), None),
    )
    return jax.shard_map(
        body, mesh=mesh, in_specs=placed, out_specs=(P(("blk", "rep"), None), P()), check_vma=False
    )
```

```python
import jax
import jax.numpy as jnp
from jax import lax
from jax.experimental import pallas as pl
from jax.experimental.pallas import tpu as pltpu
from jax.sharding import PartitionSpec as P

NX, NY, NZ, NC = 4, 4, 8, 2
BOTH = ("blk", "rep")
UNROLL = 8


def flat_index(x, y, z, core):
    return (((x // 2) * NY + y) * NC + core) * (2 * NZ) + (x % 2) * NZ + z


def pairs(move):
    result = []
    for x in range(NX):
        for y in range(NY):
            for z in range(NZ):
                for core in range(NC):
                    tx, ty, tz, tc = move(x, y, z, core)
                    result.append((flat_index(x, y, z, core), flat_index(tx % NX, ty % NY, tz % NZ, tc)))
    return result


def along_z(step):
    return pairs(lambda x, y, z, core: (x, y, z + step, core))


def along_q(step):
    return pairs(lambda x, y, z, core: (x + step * core, y + step * (1 - core), z, core))


def along_s(step):
    return pairs(lambda x, y, z, core: (x + step * (1 - core), y + step * core, z, core))


def spread_over(value, places):
    count = len(places[0])
    copies = jnp.broadcast_to(value[None], (count, *value.shape))
    return lax.all_to_all(copies, BOTH, 0, 0, axis_index_groups=places, tiled=True)


def z_lines():
    return [[flat_index(x, y, z, c) for z in range(NZ)] for x in range(NX) for y in range(NY) for c in range(NC)]


def opposite_x():
    return pairs(lambda x, y, z, core: (x + 2, y, z, core))


def paired_y(bit):
    return pairs(lambda x, y, z, core: (x, y ^ bit, z, core))


def across_x():
    return pairs(lambda x, y, z, core: (x + 1 - 2 * (x % 2), y, z, core))


def other_core():
    return pairs(lambda x, y, z, core: (x, y, z, 1 - core))


def send(value, moves):
    return lax.ppermute(value, BOTH, moves)


def ring_first(value, along):
    return send(value, along(1)), send(value, along(-1))


def ring_last(behind, ahead, along):
    half = behind.shape[0] // 2
    return [send(behind[:half], along(1)), send(ahead[half:], along(-1))]


def together(*values):
    return lax.optimization_barrier(values)


def stacked(found):
    return jnp.stack([part[0] if len(part) == 1 else jnp.concatenate(part, axis=0) for part in found])


def products_kernel(places, counts, unit0, unit1, columns, here, kept, received, *rest):
    chunks = rest[: len(places)]
    own_out, other_out, units, totals, sem = rest[len(places):]
    step = pl.program_id(0)

    @pl.when(step == 0)
    def _():
        copies = [
            pltpu.make_async_copy(chunk.at[pl.ds(0, size)], units.at[pl.ds(start, size)], sem.at[n])
            for n, (chunk, (start, size)) in enumerate(zip(chunks, places))
        ]
        for copy in copies:
            copy.start()
        totals[...] = jnp.zeros_like(totals)
        for copy in copies:
            copy.wait()

    slots = kept.shape[2]
    for side, tiles in ((0, kept), (1, received)):
        base = (side * pl.num_programs(0) + step) * slots

        def batch(i, _):
            found = []
            for k in range(UNROLL):
                slot = i * UNROLL + k
                entry = base + slot
                tile = tiles[0, 0, slot] if side == 0 else tiles[0, slot]
                rows = jnp.concatenate([units[unit0[entry]], units[unit1[entry]]], axis=0)
                found.append((columns[entry], lax.dot_general(
                    tile, rows, (((0,), (0,)), ((), ())), preferred_element_type=jnp.float32)))
            for column, product in found:
                totals[column] += product
            return 0

        live = counts[side * pl.num_programs(0) + step]
        lax.fori_loop(0, (live + UNROLL - 1) // UNROLL, batch, 0)

    @pl.when(step == pl.num_programs(0) - 1)
    def _():
        half = own_out.shape[0]
        own_out[...] = totals[:half]
        other_out[...] = totals[half:].astype(other_out.dtype)


def features_kernel(places, here, partial, *rest):
    pieces = rest[: len(places)]
    gradient, features, sem = rest[len(places):]
    step = pl.program_id(0)

    @pl.when(step == 0)
    def _():
        copies = [
            pltpu.make_async_copy(piece.at[pl.ds(start, features.shape[1])], features.at[n], sem.at[n])
            for n, (piece, start) in enumerate(zip(pieces, places))
        ]
        for copy in copies:
            copy.start()
        gradient[...] = jnp.zeros_like(gradient)
        for copy in copies:
            copy.wait()

    total = gradient[...]
    for part in range(2):
        place = 2 * step + part
        ahead = lax.rem(place - here[2] + NZ, NZ)
        for low in range(2):
            near = lax.bitwise_xor(low, here[1])
            lanes = jnp.concatenate([features[ahead, 3 * near + n] for n in range(3)], axis=0)
            total += lax.dot_general(
                lanes, partial[low, part], (((0,), (0,)), ((), ())), preferred_element_type=jnp.float32)
    gradient[...] = total


def features_product(partial, pieces, places, here):
    width = partial.shape[-1]
    return pl.pallas_call(
        lambda *refs: features_kernel(places, *refs),
        out_shape=jax.ShapeDtypeStruct((width, width), jnp.float32),
        grid_spec=pltpu.PrefetchScalarGridSpec(
            num_scalar_prefetch=1,
            grid=(NZ // 2,),
            in_specs=[pl.BlockSpec((2, 2, 192, width), lambda d, here: (0, d, 0, 0))]
            + [pl.BlockSpec(memory_space=pl.ANY)] * NZ,
            out_specs=pl.BlockSpec((width, width), lambda d, here: (0, 0)),
            scratch_shapes=[pltpu.VMEM((NZ, 6, 64, width), jnp.bfloat16), pltpu.SemaphoreType.DMA((NZ,))],
        ),
        compiler_params=pltpu.CompilerParams(vmem_limit_bytes=56 << 20),
        cost_estimate=pl.CostEstimate(flops=2 * 3072 * width * width, bytes_accessed=4 << 20, transcendentals=0),
        name="features_product",
    )(here, partial, *pieces)


def pick_kernel(side, tiles, picked, held, in_sem, out_sem):
    groups = range(picked.shape[0])
    reads = [pltpu.make_async_copy(tiles.at[g, side[0]], held.at[g], in_sem.at[g]) for g in groups]
    writes = [pltpu.make_async_copy(held.at[g], picked.at[g], out_sem.at[g]) for g in groups]
    for read in reads:
        read.start()
    for read, write in zip(reads, writes):
        read.wait()
        write.start()
    for write in writes:
        write.wait()


def pick(tiles, side):
    groups, _, slots, block, _ = tiles.shape
    return pl.pallas_call(
        pick_kernel,
        out_shape=jax.ShapeDtypeStruct((groups, slots, block, block), tiles.dtype),
        grid_spec=pltpu.PrefetchScalarGridSpec(
            num_scalar_prefetch=1,
            grid=(),
            in_specs=[pl.BlockSpec(memory_space=pl.ANY)],
            out_specs=pl.BlockSpec(memory_space=pl.ANY),
            scratch_shapes=[
                pltpu.VMEM((groups, slots, block, block), tiles.dtype),
                pltpu.SemaphoreType.DMA((groups,)),
                pltpu.SemaphoreType.DMA((groups,)),
            ],
        ),
        compiler_params=pltpu.CompilerParams(vmem_limit_bytes=56 << 20),
        cost_estimate=pl.CostEstimate(flops=0, bytes_accessed=12 << 20, transcendentals=0),
        name="pick_tiles",
    )(side.reshape(1).astype(jnp.int32), tiles)


def products(tiles, received, chunks, places, counts, unit0, unit1, columns, here):
    groups, _, slots, block, _ = tiles.shape
    width = chunks[0].shape[-1]
    return pl.pallas_call(
        lambda *refs: products_kernel(places, *refs),
        out_shape=(
            jax.ShapeDtypeStruct((24, block, width), jnp.float32),
            jax.ShapeDtypeStruct((24, block, width), jnp.bfloat16),
        ),
        grid_spec=pltpu.PrefetchScalarGridSpec(
            num_scalar_prefetch=5,
            grid=(groups,),
            in_specs=[
                pl.BlockSpec((1, 1, slots, block, block), lambda g, n, u, v, k, here: (g, here[0], 0, 0, 0)),
                pl.BlockSpec((1, slots, block, block), lambda g, *_: (g, 0, 0, 0)),
            ] + [pl.BlockSpec(memory_space=pl.ANY)] * len(chunks),
            out_specs=(pl.BlockSpec((24, block, width), lambda g, *_: (0, 0, 0)),) * 2,
            scratch_shapes=[
                pltpu.VMEM((384, 64, width), jnp.bfloat16),
                pltpu.VMEM((48, block, width), jnp.float32),
                pltpu.SemaphoreType.DMA((len(chunks),)),
            ],
        ),
        compiler_params=pltpu.CompilerParams(vmem_limit_bytes=56 << 20),
        cost_estimate=pl.CostEstimate(flops=384 * 2 * block * block * width, bytes_accessed=30 << 20, transcendentals=0),
        name="tile_products",
    )(counts, unit0, unit1, columns, here, tiles, received, *chunks)


def body(out_grad, pre_act, features, weight, degrees, tiles, tile_rows, tile_cols):
    own_blk, own_rep = lax.axis_index("blk"), lax.axis_index("rep")
    core, y = own_blk % NC, (own_blk // NC) % NY
    x = (own_blk // (NC * NY)) * 2 + own_rep // NZ
    z = own_rep % NZ
    width = out_grad.shape[1]
    slots, block = tiles.shape[1], tiles.shape[2]
    groups = tiles.shape[0] // NC

    inverse_root = lax.rsqrt(degrees.astype(jnp.float32))
    active = (pre_act > 0).astype(jnp.float32)
    scaled = (out_grad.astype(jnp.float32) * active * inverse_root[:, None]).astype(jnp.bfloat16)

    rooted_features = (features.astype(jnp.float32) * inverse_root[:, None]).astype(jnp.bfloat16)

    odd = own_rep % 2
    full = lax.dynamic_slice_in_dim(scaled, odd * 64, 128, 0)
    half = lax.dynamic_slice_in_dim(scaled, (1 - odd) * 128, 64, 0)

    flip = other_core()
    by_parity = tiles.reshape(groups, NC, slots, block, block)
    codes = (tile_rows * 32 + tile_cols).reshape(groups, NC, slots)
    kept_codes = lax.dynamic_index_in_dim(codes, core, 1, keepdims=False)
    received_codes = send(lax.dynamic_index_in_dim(codes, 1 - core, 1, keepdims=False), flip)
    far_features = send(rooted_features, across_x())
    full_line = spread_over(full, z_lines())
    half_line = jnp.stack([half] + [send(half, along_s(-d)) for d in (1, 2, 3)])
    half_q = [half_line] + [send(half_line, along_q(-d)) for d in (1, 2, 3)]
    half_q[1], side = together(half_q[1], 1 - core)
    picked = pick(by_parity, side)
    half_plane = jnp.concatenate(
        half_q + [rooted_features.reshape(-1, 64, width), far_features.reshape(-1, 64, width)])
    half_z = {0: [half_plane]}
    behind, ahead = ring_first(half_plane, along_z)
    half_z[7], half_z[1] = [behind], [ahead]
    full_q = {0: [full_line]}
    q_behind, q_ahead = ring_first(full_line, along_q)
    q_behind, q_ahead, behind, ahead = together(q_behind, q_ahead, behind, ahead)
    full_q[3], full_q[1], full_q[2] = [q_behind], [q_ahead], ring_last(q_behind, q_ahead, along_q)
    full_plane = stacked([full_q[d] for d in range(4)])
    full_plane, picked = together(full_plane, picked)
    received = send(picked, flip)
    first, second = full_plane[:2], full_plane[2:]
    first_behind, second_ahead = send(first, along_s(1)), send(second, along_s(-1))
    second_behind, first_ahead = send(second, along_s(1)), send(first, along_s(-1))
    full_s = [[first, second], [first_ahead, second_ahead],
              [send(first_behind, along_s(1)), send(second_ahead, along_s(-1))], [first_behind, second_behind]]
    for d in (2, 3):
        behind, ahead = send(behind, along_z(1)), send(ahead, along_z(-1))
        if d == 2:
            behind, ahead, received = together(behind, ahead, received)
        half_z[NZ - d], half_z[d] = [behind], [ahead]
    half_z[4] = ring_last(behind, ahead, along_z)
    full_found = full_s
    half_found = [half_z[d] for d in range(NZ)]

    codes = jnp.stack([kept_codes, received_codes])
    rows, cols = codes // 32, codes % 32

    group = jnp.arange(groups)[None, :, None] * NC
    pair, kind = rows // 3, rows % 3
    source_x = (group // (NC * NY)) * 2 + (2 * pair) // NZ
    source_y = (group // NC) % NY
    ahead_x, ahead_y = (source_x - x) % NX, (source_y - y) % NY
    ahead_s = jnp.where(core == 0, ahead_x, ahead_y)
    ahead_q = jnp.where(core == 0, ahead_y, ahead_x)
    first_z, second_z = (2 * pair - z) % NZ, (2 * pair + 1 - z) % NZ
    full_unit = ((ahead_s * 4 + ahead_q) * NZ + (2 * pair + kind // 2) % NZ) * 2
    half_unit = 256 + ahead_q * 4 + ahead_s
    split = kind == 1
    unit0 = jnp.where(split, half_unit + first_z * 16, full_unit).reshape(-1).astype(jnp.int32)
    unit1 = jnp.where(split, half_unit + second_z * 16, full_unit + 1).reshape(-1).astype(jnp.int32)
    columns = (cols + jnp.arange(2)[:, None, None] * 24).reshape(-1).astype(jnp.int32)
    last = jnp.max(jnp.where(codes != 0, jnp.arange(slots) + 1, 0), axis=2)
    counts = jnp.minimum(last + 1, slots).reshape(-1).astype(jnp.int32)

    chunks, places, at = [], [], 0
    for part in (piece for found in full_found for piece in found):
        chunks.append(part.reshape(-1, 64, width))
        places.append((at, chunks[-1].shape[0]))
        at += chunks[-1].shape[0]
    feature_pieces, feature_places = [], []
    for found in half_found:
        left = 16
        for piece in found:
            count = min(left, piece.shape[0])
            chunks.append(piece)
            places.append((at, count))
            at, left = at + count, left - count
            last_piece, last_count = piece, count
        feature_pieces.append(last_piece)
        feature_places.append(last_count)

    here = jnp.stack([core, own_rep // NZ, z]).astype(jnp.int32)
    own, other = products(by_parity, received, chunks, places, counts, unit0, unit1, columns, here)
    partial = (own + send(other, flip).astype(jnp.float32)).astype(jnp.bfloat16).reshape(2, NZ, -1, width)
    local_weight = features_product(partial, feature_pieces, feature_places, here)
    near = lax.dynamic_index_in_dim(partial, own_rep // NZ, 0, keepdims=False)
    across = send(lax.dynamic_index_in_dim(partial, 1 - own_rep // NZ, 0, keepdims=False), across_x())
    own_rows = lax.all_to_all(local_weight, "rep", 0, 0, tiled=True).reshape(16, 16, width).sum(axis=0)
    line = (near.astype(jnp.float32) + across.astype(jnp.float32)).astype(jnp.bfloat16)
    line, own_rows = together(line, own_rows)
    terms = lax.all_to_all(line, BOTH, 0, 0, axis_index_groups=z_lines(), tiled=True)
    for partner in (other_core(), opposite_x(), paired_y(1), paired_y(2)):
        own_rows = own_rows + send(own_rows, partner)
    own_rows, terms = together(own_rows, terms)
    spread = jnp.broadcast_to(own_rows[None], (16, 16, width)).reshape(256, width)
    weight_grad = lax.all_to_all(spread, "rep", 0, 0, tiled=True)
    summed = terms.astype(jnp.float32).sum(axis=0)

    propagated = (inverse_root[:, None] * summed).astype(jnp.bfloat16)
    input_grad = lax.dot_general(
        propagated, weight, (((1,), (1,)), ((), ())), preferred_element_type=jnp.float32
    ).astype(jnp.bfloat16)
    return (input_grad, weight_grad)


def solution(mesh):
    placed = (
        P(("blk", "rep"), None),
        P(("blk", "rep"), None),
        P(("blk", "rep"), None),
        P(),
        P(("blk", "rep")),
        P(("blk", "rep"), None, None, None),
        P(("blk", "rep"), None),
        P(("blk", "rep"), None),
    )
    return jax.shard_map(
        body, mesh=mesh, in_specs=placed, out_specs=(P(("blk", "rep"), None), P()), check_vma=False
    )
```

```python
import jax
import jax.numpy as jnp
from jax import lax
from jax.experimental import pallas as pl
from jax.experimental.pallas import tpu as pltpu
from jax.sharding import PartitionSpec as P

NX, NY, NZ, NC = 4, 4, 8, 2
BOTH = ("blk", "rep")
UNROLL = 8


def flat_index(x, y, z, core):
    return (((x // 2) * NY + y) * NC + core) * (2 * NZ) + (x % 2) * NZ + z


def pairs(move):
    result = []
    for x in range(NX):
        for y in range(NY):
            for z in range(NZ):
                for core in range(NC):
                    tx, ty, tz, tc = move(x, y, z, core)
                    result.append((flat_index(x, y, z, core), flat_index(tx % NX, ty % NY, tz % NZ, tc)))
    return result


def along_z(step):
    return pairs(lambda x, y, z, core: (x, y, z + step, core))


def along_q(step):
    return pairs(lambda x, y, z, core: (x + step * core, y + step * (1 - core), z, core))


def along_s(step):
    return pairs(lambda x, y, z, core: (x + step * (1 - core), y + step * core, z, core))


def spread_over(value, places):
    count = len(places[0])
    copies = jnp.broadcast_to(value[None], (count, *value.shape))
    return lax.all_to_all(copies, BOTH, 0, 0, axis_index_groups=places, tiled=True)


def z_lines():
    return [[flat_index(x, y, z, c) for z in range(NZ)] for x in range(NX) for y in range(NY) for c in range(NC)]


def opposite_x():
    return pairs(lambda x, y, z, core: (x + 2, y, z, core))


def paired_y(bit):
    return pairs(lambda x, y, z, core: (x, y ^ bit, z, core))


def across_x():
    return pairs(lambda x, y, z, core: (x + 1 - 2 * (x % 2), y, z, core))


def other_core():
    return pairs(lambda x, y, z, core: (x, y, z, 1 - core))


def send(value, moves):
    return lax.ppermute(value, BOTH, moves)


def ring_first(value, along):
    return send(value, along(1)), send(value, along(-1))


def ring_last(behind, ahead, along):
    half = behind.shape[0] // 2
    return [send(behind[:half], along(1)), send(ahead[half:], along(-1))]


def together(*values):
    return lax.optimization_barrier(values)


def stacked(found):
    return jnp.stack([part[0] if len(part) == 1 else jnp.concatenate(part, axis=0) for part in found])


def products_kernel(places, counts, unit0, unit1, columns, here, kept, received, *rest):
    chunks = rest[: len(places)]
    own_out, other_out, units, totals, sem = rest[len(places):]
    step = pl.program_id(0)

    @pl.when(step == 0)
    def _():
        copies = [
            pltpu.make_async_copy(chunk.at[pl.ds(0, size)], units.at[pl.ds(start, size)], sem.at[n])
            for n, (chunk, (start, size)) in enumerate(zip(chunks, places))
        ]
        for copy in copies:
            copy.start()
        totals[...] = jnp.zeros_like(totals)
        for copy in copies:
            copy.wait()

    slots = kept.shape[2]
    starts = [(side * pl.num_programs(0) + step) * slots for side in range(2)]

    def batch(i, _):
        found = []
        for side, base in enumerate(starts):
            for k in range(UNROLL):
                slot = i * UNROLL + k
                entry = base + slot
                tile = received[0, slot] if side else kept[0, 0, slot]
                rows = jnp.concatenate([units[unit0[entry]], units[unit1[entry]]], axis=0)
                found.append((columns[entry], lax.dot_general(
                    tile, rows, (((0,), (0,)), ((), ())), preferred_element_type=jnp.float32)))
        for column, product in found:
            totals[column] += product
        return 0

    live = jnp.maximum(counts[step], counts[pl.num_programs(0) + step])
    lax.fori_loop(0, (live + UNROLL - 1) // UNROLL, batch, 0)

    @pl.when(step == pl.num_programs(0) - 1)
    def _():
        half = own_out.shape[0]
        own_out[...] = totals[:half]
        other_out[...] = totals[half:].astype(other_out.dtype)


def features_kernel(places, here, partial, *rest):
    pieces = rest[: len(places)]
    gradient, features, sem = rest[len(places):]
    step = pl.program_id(0)

    @pl.when(step == 0)
    def _():
        copies = [
            pltpu.make_async_copy(piece.at[pl.ds(start, features.shape[1])], features.at[n], sem.at[n])
            for n, (piece, start) in enumerate(zip(pieces, places))
        ]
        for copy in copies:
            copy.start()
        gradient[...] = jnp.zeros_like(gradient)
        for copy in copies:
            copy.wait()

    total = gradient[...]
    for part in range(2):
        place = 2 * step + part
        ahead = lax.rem(place - here[2] + NZ, NZ)
        for low in range(2):
            near = lax.bitwise_xor(low, here[1])
            lanes = jnp.concatenate([features[ahead, 3 * near + n] for n in range(3)], axis=0)
            total += lax.dot_general(
                lanes, partial[low, part], (((0,), (0,)), ((), ())), preferred_element_type=jnp.float32)
    gradient[...] = total


def features_product(partial, pieces, places, here):
    width = partial.shape[-1]
    return pl.pallas_call(
        lambda *refs: features_kernel(places, *refs),
        out_shape=jax.ShapeDtypeStruct((width, width), jnp.float32),
        grid_spec=pltpu.PrefetchScalarGridSpec(
            num_scalar_prefetch=1,
            grid=(NZ // 2,),
            in_specs=[pl.BlockSpec((2, 2, 192, width), lambda d, here: (0, d, 0, 0))]
            + [pl.BlockSpec(memory_space=pl.ANY)] * NZ,
            out_specs=pl.BlockSpec((width, width), lambda d, here: (0, 0)),
            scratch_shapes=[pltpu.VMEM((NZ, 6, 64, width), jnp.bfloat16), pltpu.SemaphoreType.DMA((NZ,))],
        ),
        compiler_params=pltpu.CompilerParams(vmem_limit_bytes=56 << 20),
        cost_estimate=pl.CostEstimate(flops=2 * 3072 * width * width, bytes_accessed=4 << 20, transcendentals=0),
        name="features_product",
    )(here, partial, *pieces)


def pick_kernel(side, tiles, picked, held, in_sem, out_sem):
    groups = range(picked.shape[0])
    reads = [pltpu.make_async_copy(tiles.at[g, side[0]], held.at[g], in_sem.at[g]) for g in groups]
    writes = [pltpu.make_async_copy(held.at[g], picked.at[g], out_sem.at[g]) for g in groups]
    for read in reads:
        read.start()
    for read, write in zip(reads, writes):
        read.wait()
        write.start()
    for write in writes:
        write.wait()


def pick(tiles, side):
    groups, _, slots, block, _ = tiles.shape
    return pl.pallas_call(
        pick_kernel,
        out_shape=jax.ShapeDtypeStruct((groups, slots, block, block), tiles.dtype),
        grid_spec=pltpu.PrefetchScalarGridSpec(
            num_scalar_prefetch=1,
            grid=(),
            in_specs=[pl.BlockSpec(memory_space=pl.ANY)],
            out_specs=pl.BlockSpec(memory_space=pl.ANY),
            scratch_shapes=[
                pltpu.VMEM((groups, slots, block, block), tiles.dtype),
                pltpu.SemaphoreType.DMA((groups,)),
                pltpu.SemaphoreType.DMA((groups,)),
            ],
        ),
        compiler_params=pltpu.CompilerParams(vmem_limit_bytes=56 << 20),
        cost_estimate=pl.CostEstimate(flops=0, bytes_accessed=12 << 20, transcendentals=0),
        name="pick_tiles",
    )(side.reshape(1).astype(jnp.int32), tiles)


def products(tiles, received, chunks, places, counts, unit0, unit1, columns, here):
    groups, _, slots, block, _ = tiles.shape
    width = chunks[0].shape[-1]
    return pl.pallas_call(
        lambda *refs: products_kernel(places, *refs),
        out_shape=(
            jax.ShapeDtypeStruct((24, block, width), jnp.float32),
            jax.ShapeDtypeStruct((24, block, width), jnp.bfloat16),
        ),
        grid_spec=pltpu.PrefetchScalarGridSpec(
            num_scalar_prefetch=5,
            grid=(groups,),
            in_specs=[
                pl.BlockSpec((1, 1, slots, block, block), lambda g, n, u, v, k, here: (g, here[0], 0, 0, 0)),
                pl.BlockSpec((1, slots, block, block), lambda g, *_: (g, 0, 0, 0)),
            ] + [pl.BlockSpec(memory_space=pl.ANY)] * len(chunks),
            out_specs=(pl.BlockSpec((24, block, width), lambda g, *_: (0, 0, 0)),) * 2,
            scratch_shapes=[
                pltpu.VMEM((384, 64, width), jnp.bfloat16),
                pltpu.VMEM((48, block, width), jnp.float32),
                pltpu.SemaphoreType.DMA((len(chunks),)),
            ],
        ),
        compiler_params=pltpu.CompilerParams(vmem_limit_bytes=56 << 20),
        cost_estimate=pl.CostEstimate(flops=384 * 2 * block * block * width, bytes_accessed=30 << 20, transcendentals=0),
        name="tile_products",
    )(counts, unit0, unit1, columns, here, tiles, received, *chunks)


def body(out_grad, pre_act, features, weight, degrees, tiles, tile_rows, tile_cols):
    own_blk, own_rep = lax.axis_index("blk"), lax.axis_index("rep")
    core, y = own_blk % NC, (own_blk // NC) % NY
    x = (own_blk // (NC * NY)) * 2 + own_rep // NZ
    z = own_rep % NZ
    width = out_grad.shape[1]
    slots, block = tiles.shape[1], tiles.shape[2]
    groups = tiles.shape[0] // NC

    inverse_root = lax.rsqrt(degrees.astype(jnp.float32))
    active = (pre_act > 0).astype(jnp.float32)
    scaled = (out_grad.astype(jnp.float32) * active * inverse_root[:, None]).astype(jnp.bfloat16)

    rooted_features = (features.astype(jnp.float32) * inverse_root[:, None]).astype(jnp.bfloat16)

    odd = own_rep % 2
    full = lax.dynamic_slice_in_dim(scaled, odd * 64, 128, 0)
    half = lax.dynamic_slice_in_dim(scaled, (1 - odd) * 128, 64, 0)

    flip = other_core()
    by_parity = tiles.reshape(groups, NC, slots, block, block)
    codes = (tile_rows * 32 + tile_cols).reshape(groups, NC, slots)
    kept_codes = lax.dynamic_index_in_dim(codes, core, 1, keepdims=False)
    received_codes = send(lax.dynamic_index_in_dim(codes, 1 - core, 1, keepdims=False), flip)
    far_features = send(rooted_features, across_x())
    full_line = spread_over(full, z_lines())
    half_line = jnp.stack([half] + [send(half, along_s(-d)) for d in (1, 2, 3)])
    half_q = [half_line] + [send(half_line, along_q(-d)) for d in (1, 2, 3)]
    half_plane = jnp.concatenate(
        half_q + [rooted_features.reshape(-1, 64, width), far_features.reshape(-1, 64, width)])
    half_z = {0: [half_plane]}
    behind, ahead = ring_first(half_plane, along_z)
    q_behind, q_ahead = ring_first(full_line, along_q)
    q_behind, q_ahead, behind, ahead, side = together(q_behind, q_ahead, behind, ahead, 1 - core)
    picked = pick(by_parity, side)
    half_z[7], half_z[1] = [behind], [ahead]
    first = jnp.stack([full_line, q_ahead])
    q_opposite = send(q_behind, along_q(1))
    first_behind, first_ahead = ring_first(first, along_s)
    behind, ahead = send(behind, along_z(1)), send(ahead, along_z(-1))
    q_opposite, first_behind, first_ahead, behind, ahead, picked = together(
        q_opposite, first_behind, first_ahead, behind, ahead, picked)
    received = send(picked, flip)
    half_z[6], half_z[2] = [behind], [ahead]
    second = jnp.stack([q_opposite, q_behind])
    second_behind, second_ahead = ring_first(second, along_s)
    behind, ahead = send(behind, along_z(1)), send(ahead, along_z(-1))
    second_behind, second_ahead, behind, ahead, received = together(
        second_behind, second_ahead, behind, ahead, received)
    half_z[5], half_z[3] = [behind], [ahead]
    half_z[4] = ring_last(behind, ahead, along_z)
    full_found = [[first, second], [first_ahead, second_ahead],
                  [send(first_behind, along_s(1)), send(second_ahead, along_s(-1))], [first_behind, second_behind]]
    half_found = [half_z[d] for d in range(NZ)]

    codes = jnp.stack([kept_codes, received_codes])
    rows, cols = codes // 32, codes % 32

    group = jnp.arange(groups)[None, :, None] * NC
    pair, kind = rows // 3, rows % 3
    source_x = (group // (NC * NY)) * 2 + (2 * pair) // NZ
    source_y = (group // NC) % NY
    ahead_x, ahead_y = (source_x - x) % NX, (source_y - y) % NY
    ahead_s = jnp.where(core == 0, ahead_x, ahead_y)
    ahead_q = jnp.where(core == 0, ahead_y, ahead_x)
    first_z, second_z = (2 * pair - z) % NZ, (2 * pair + 1 - z) % NZ
    full_unit = ((ahead_s * 4 + ahead_q) * NZ + (2 * pair + kind // 2) % NZ) * 2
    half_unit = 256 + ahead_q * 4 + ahead_s
    split = kind == 1
    unit0 = jnp.where(split, half_unit + first_z * 16, full_unit).reshape(-1).astype(jnp.int32)
    unit1 = jnp.where(split, half_unit + second_z * 16, full_unit + 1).reshape(-1).astype(jnp.int32)
    columns = (cols + jnp.arange(2)[:, None, None] * 24).reshape(-1).astype(jnp.int32)
    last = jnp.max(jnp.where(codes != 0, jnp.arange(slots) + 1, 0), axis=2)
    counts = jnp.minimum(last + 1, slots).reshape(-1).astype(jnp.int32)

    chunks, places, at = [], [], 0
    for part in (piece for found in full_found for piece in found):
        chunks.append(part.reshape(-1, 64, width))
        places.append((at, chunks[-1].shape[0]))
        at += chunks[-1].shape[0]
    feature_pieces, feature_places = [], []
    for found in half_found:
        left = 16
        for piece in found:
            count = min(left, piece.shape[0])
            chunks.append(piece)
            places.append((at, count))
            at, left = at + count, left - count
            last_piece, last_count = piece, count
        feature_pieces.append(last_piece)
        feature_places.append(last_count)

    here = jnp.stack([core, own_rep // NZ, z]).astype(jnp.int32)
    own, other = products(by_parity, received, chunks, places, counts, unit0, unit1, columns, here)
    partial = (own + send(other, flip).astype(jnp.float32)).astype(jnp.bfloat16).reshape(2, NZ, -1, width)
    local_weight = features_product(partial, feature_pieces, feature_places, here)
    near = lax.dynamic_index_in_dim(partial, own_rep // NZ, 0, keepdims=False)
    across = send(lax.dynamic_index_in_dim(partial, 1 - own_rep // NZ, 0, keepdims=False), across_x())
    own_rows = lax.all_to_all(local_weight, "rep", 0, 0, tiled=True).reshape(16, 16, width).sum(axis=0)
    line = (near.astype(jnp.float32) + across.astype(jnp.float32)).astype(jnp.bfloat16)
    line, own_rows = together(line, own_rows)
    terms = lax.all_to_all(line, BOTH, 0, 0, axis_index_groups=z_lines(), tiled=True)
    for partner in (other_core(), opposite_x(), paired_y(1), paired_y(2)):
        own_rows = own_rows + send(own_rows, partner)
    own_rows, terms = together(own_rows, terms)
    spread = jnp.broadcast_to(own_rows[None], (16, 16, width)).reshape(256, width)
    weight_grad = lax.all_to_all(spread, "rep", 0, 0, tiled=True)
    summed = terms.astype(jnp.float32).sum(axis=0)

    propagated = (inverse_root[:, None] * summed).astype(jnp.bfloat16)
    input_grad = lax.dot_general(
        propagated, weight, (((1,), (1,)), ((), ())), preferred_element_type=jnp.float32
    ).astype(jnp.bfloat16)
    return (input_grad, weight_grad)


def solution(mesh):
    placed = (
        P(("blk", "rep"), None),
        P(("blk", "rep"), None),
        P(("blk", "rep"), None),
        P(),
        P(("blk", "rep")),
        P(("blk", "rep"), None, None, None),
        P(("blk", "rep"), None),
        P(("blk", "rep"), None),
    )
    return jax.shard_map(
        body, mesh=mesh, in_specs=placed, out_specs=(P(("blk", "rep"), None), P()), check_vma=False
    )
```

```python
import jax
import jax.numpy as jnp
from jax import lax
from jax.experimental import pallas as pl
from jax.experimental.pallas import tpu as pltpu
from jax.sharding import PartitionSpec as P

NX, NY, NZ, NC = 4, 4, 8, 2
BOTH = ("blk", "rep")
UNROLL = 8


def flat_index(x, y, z, core):
    return (((x // 2) * NY + y) * NC + core) * (2 * NZ) + (x % 2) * NZ + z


def pairs(move):
    result = []
    for x in range(NX):
        for y in range(NY):
            for z in range(NZ):
                for core in range(NC):
                    tx, ty, tz, tc = move(x, y, z, core)
                    result.append((flat_index(x, y, z, core), flat_index(tx % NX, ty % NY, tz % NZ, tc)))
    return result


def along_z(step):
    return pairs(lambda x, y, z, core: (x, y, z + step, core))


def along_q(step):
    return pairs(lambda x, y, z, core: (x + step * core, y + step * (1 - core), z, core))


def along_s(step):
    return pairs(lambda x, y, z, core: (x + step * (1 - core), y + step * core, z, core))


def spread_over(value, places):
    count = len(places[0])
    copies = jnp.broadcast_to(value[None], (count, *value.shape))
    return lax.all_to_all(copies, BOTH, 0, 0, axis_index_groups=places, tiled=True)


def z_lines():
    return [[flat_index(x, y, z, c) for z in range(NZ)] for x in range(NX) for y in range(NY) for c in range(NC)]


def opposite_x():
    return pairs(lambda x, y, z, core: (x + 2, y, z, core))


def paired_y(bit):
    return pairs(lambda x, y, z, core: (x, y ^ bit, z, core))


def across_x():
    return pairs(lambda x, y, z, core: (x + 1 - 2 * (x % 2), y, z, core))


def other_core():
    return pairs(lambda x, y, z, core: (x, y, z, 1 - core))


def send(value, moves):
    return lax.ppermute(value, BOTH, moves)


def ring_first(value, along):
    return send(value, along(1)), send(value, along(-1))


def ring_last(behind, ahead, along):
    half = behind.shape[0] // 2
    return [send(behind[:half], along(1)), send(ahead[half:], along(-1))]


def together(*values):
    return lax.optimization_barrier(values)


def stacked(found):
    return jnp.stack([part[0] if len(part) == 1 else jnp.concatenate(part, axis=0) for part in found])


def products_kernel(places, counts, unit0, unit1, columns, here, kept, received, *rest):
    chunks = rest[: len(places)]
    own_out, other_out, units, totals, sem = rest[len(places):]
    step = pl.program_id(0)

    @pl.when(step == 0)
    def _():
        copies = [
            pltpu.make_async_copy(chunk.at[pl.ds(0, size)], units.at[pl.ds(start, size)], sem.at[n])
            for n, (chunk, (start, size)) in enumerate(zip(chunks, places))
        ]
        for copy in copies:
            copy.start()
        totals[...] = jnp.zeros_like(totals)
        for copy in copies:
            copy.wait()

    slots = kept.shape[2]
    starts = [(side * pl.num_programs(0) + step) * slots for side in range(2)]

    def batch(i, _):
        found = []
        for side, base in enumerate(starts):
            for k in range(UNROLL):
                slot = i * UNROLL + k
                entry = base + slot
                tile = received[0, slot] if side else kept[0, 0, slot]
                rows = jnp.concatenate([units[unit0[entry]], units[unit1[entry]]], axis=0)
                found.append((columns[entry], lax.dot_general(
                    tile, rows, (((0,), (0,)), ((), ())), preferred_element_type=jnp.float32)))
        for column, product in found:
            totals[column] += product
        return 0

    live = jnp.maximum(counts[step], counts[pl.num_programs(0) + step])
    lax.fori_loop(0, (live + UNROLL - 1) // UNROLL, batch, 0)

    @pl.when(step == pl.num_programs(0) - 1)
    def _():
        half = own_out.shape[0]
        own_out[...] = totals[:half]
        other_out[...] = totals[half:].astype(other_out.dtype)


def turn_kernel(places, *rest):
    pieces = rest[: len(places)]
    turned, held, sem = rest[len(places):]
    copies = [
        pltpu.make_async_copy(piece.at[pl.ds(start, held.shape[1])], held.at[n], sem.at[n])
        for n, (piece, start) in enumerate(zip(pieces, places))
    ]
    for copy in copies:
        copy.start()
    for n, copy in enumerate(copies):
        copy.wait()
        turned[n] = jnp.concatenate([held[n, k] for k in range(held.shape[1])], axis=0).T


def turn_features(pieces, places):
    width = pieces[0].shape[-1]
    return pl.pallas_call(
        lambda *refs: turn_kernel(places, *refs),
        out_shape=jax.ShapeDtypeStruct((NZ, width, 384), jnp.bfloat16),
        grid_spec=pltpu.PrefetchScalarGridSpec(
            num_scalar_prefetch=0,
            grid=(),
            in_specs=[pl.BlockSpec(memory_space=pl.ANY)] * NZ,
            out_specs=pl.BlockSpec(memory_space=pltpu.VMEM),
            scratch_shapes=[pltpu.VMEM((NZ, 6, 64, width), jnp.bfloat16), pltpu.SemaphoreType.DMA((NZ,))],
        ),
        compiler_params=pltpu.CompilerParams(vmem_limit_bytes=56 << 20),
        cost_estimate=pl.CostEstimate(flops=0, bytes_accessed=4 << 20, transcendentals=0),
        name="turn_features",
    )(*pieces)


def features_kernel(here, turned, partial, gradient):
    @pl.when(pl.program_id(0) == 0)
    def _():
        gradient[...] = jnp.zeros_like(gradient)

    rows = jnp.concatenate([partial[here[1], 0], partial[1 - here[1], 0]], axis=0)
    gradient[...] += jnp.dot(turned[0], rows, preferred_element_type=jnp.float32)


def features_product(partial, turned, here):
    width = partial.shape[-1]
    return pl.pallas_call(
        features_kernel,
        out_shape=jax.ShapeDtypeStruct((width, width), jnp.float32),
        grid_spec=pltpu.PrefetchScalarGridSpec(
            num_scalar_prefetch=1,
            grid=(NZ,),
            in_specs=[
                pl.BlockSpec((1, width, 384), lambda d, here: (lax.rem(d - here[2] + NZ, NZ), 0, 0)),
                pl.BlockSpec((2, 1, 192, width), lambda d, here: (0, d, 0, 0)),
            ],
            out_specs=pl.BlockSpec((width, width), lambda d, here: (0, 0)),
        ),
        compiler_params=pltpu.CompilerParams(vmem_limit_bytes=56 << 20),
        cost_estimate=pl.CostEstimate(flops=2 * 3072 * width * width, bytes_accessed=4 << 20, transcendentals=0),
        name="features_product",
    )(here, turned, partial)


def pick_kernel(side, tiles, picked, held, in_sem, out_sem):
    groups = range(picked.shape[0])
    reads = [pltpu.make_async_copy(tiles.at[g, side[0]], held.at[g], in_sem.at[g]) for g in groups]
    writes = [pltpu.make_async_copy(held.at[g], picked.at[g], out_sem.at[g]) for g in groups]
    for read in reads:
        read.start()
    for read, write in zip(reads, writes):
        read.wait()
        write.start()
    for write in writes:
        write.wait()


def pick(tiles, side):
    groups, _, slots, block, _ = tiles.shape
    return pl.pallas_call(
        pick_kernel,
        out_shape=jax.ShapeDtypeStruct((groups, slots, block, block), tiles.dtype),
        grid_spec=pltpu.PrefetchScalarGridSpec(
            num_scalar_prefetch=1,
            grid=(),
            in_specs=[pl.BlockSpec(memory_space=pl.ANY)],
            out_specs=pl.BlockSpec(memory_space=pl.ANY),
            scratch_shapes=[
                pltpu.VMEM((groups, slots, block, block), tiles.dtype),
                pltpu.SemaphoreType.DMA((groups,)),
                pltpu.SemaphoreType.DMA((groups,)),
            ],
        ),
        compiler_params=pltpu.CompilerParams(vmem_limit_bytes=56 << 20),
        cost_estimate=pl.CostEstimate(flops=0, bytes_accessed=12 << 20, transcendentals=0),
        name="pick_tiles",
    )(side.reshape(1).astype(jnp.int32), tiles)


def products(tiles, received, chunks, places, counts, unit0, unit1, columns, here):
    groups, _, slots, block, _ = tiles.shape
    width = chunks[0].shape[-1]
    return pl.pallas_call(
        lambda *refs: products_kernel(places, *refs),
        out_shape=(
            jax.ShapeDtypeStruct((24, block, width), jnp.float32),
            jax.ShapeDtypeStruct((24, block, width), jnp.bfloat16),
        ),
        grid_spec=pltpu.PrefetchScalarGridSpec(
            num_scalar_prefetch=5,
            grid=(groups,),
            in_specs=[
                pl.BlockSpec((1, 1, slots, block, block), lambda g, n, u, v, k, here: (g, here[0], 0, 0, 0)),
                pl.BlockSpec((1, slots, block, block), lambda g, *_: (g, 0, 0, 0)),
            ] + [pl.BlockSpec(memory_space=pl.ANY)] * len(chunks),
            out_specs=(pl.BlockSpec((24, block, width), lambda g, *_: (0, 0, 0)),) * 2,
            scratch_shapes=[
                pltpu.VMEM((384, 64, width), jnp.bfloat16),
                pltpu.VMEM((48, block, width), jnp.float32),
                pltpu.SemaphoreType.DMA((len(chunks),)),
            ],
        ),
        compiler_params=pltpu.CompilerParams(vmem_limit_bytes=56 << 20),
        cost_estimate=pl.CostEstimate(flops=384 * 2 * block * block * width, bytes_accessed=30 << 20, transcendentals=0),
        name="tile_products",
    )(counts, unit0, unit1, columns, here, tiles, received, *chunks)


def body(out_grad, pre_act, features, weight, degrees, tiles, tile_rows, tile_cols):
    own_blk, own_rep = lax.axis_index("blk"), lax.axis_index("rep")
    core, y = own_blk % NC, (own_blk // NC) % NY
    x = (own_blk // (NC * NY)) * 2 + own_rep // NZ
    z = own_rep % NZ
    width = out_grad.shape[1]
    slots, block = tiles.shape[1], tiles.shape[2]
    groups = tiles.shape[0] // NC

    inverse_root = lax.rsqrt(degrees.astype(jnp.float32))
    active = (pre_act > 0).astype(jnp.float32)
    scaled = (out_grad.astype(jnp.float32) * active * inverse_root[:, None]).astype(jnp.bfloat16)

    rooted_features = (features.astype(jnp.float32) * inverse_root[:, None]).astype(jnp.bfloat16)

    odd = own_rep % 2
    full = lax.dynamic_slice_in_dim(scaled, odd * 64, 128, 0)
    half = lax.dynamic_slice_in_dim(scaled, (1 - odd) * 128, 64, 0)

    flip = other_core()
    by_parity = tiles.reshape(groups, NC, slots, block, block)
    codes = (tile_rows * 32 + tile_cols).reshape(groups, NC, slots)
    kept_codes = lax.dynamic_index_in_dim(codes, core, 1, keepdims=False)
    received_codes = send(lax.dynamic_index_in_dim(codes, 1 - core, 1, keepdims=False), flip)
    far_features = send(rooted_features, across_x())
    full_line = spread_over(full, z_lines())
    half_line = jnp.stack([half] + [send(half, along_s(-d)) for d in (1, 2, 3)])
    half_q = [half_line] + [send(half_line, along_q(-d)) for d in (1, 2, 3)]
    half_plane = jnp.concatenate(
        half_q + [rooted_features.reshape(-1, 64, width), far_features.reshape(-1, 64, width)])
    half_z = {0: [half_plane]}
    behind, ahead = ring_first(half_plane, along_z)
    q_behind, q_ahead = ring_first(full_line, along_q)
    q_behind, q_ahead, behind, ahead, side = together(q_behind, q_ahead, behind, ahead, 1 - core)
    picked = pick(by_parity, side)
    half_z[7], half_z[1] = [behind], [ahead]
    first = jnp.stack([full_line, q_ahead])
    q_opposite = send(q_behind, along_q(1))
    first_behind, first_ahead = ring_first(first, along_s)
    behind, ahead = send(behind, along_z(1)), send(ahead, along_z(-1))
    q_opposite, first_behind, first_ahead, behind, ahead, picked = together(
        q_opposite, first_behind, first_ahead, behind, ahead, picked)
    received = send(picked, flip)
    half_z[6], half_z[2] = [behind], [ahead]
    second = jnp.stack([q_opposite, q_behind])
    second_behind, second_ahead = ring_first(second, along_s)
    behind, ahead = send(behind, along_z(1)), send(ahead, along_z(-1))
    second_behind, second_ahead, behind, ahead, received = together(
        second_behind, second_ahead, behind, ahead, received)
    half_z[5], half_z[3] = [behind], [ahead]
    half_z[4] = ring_last(behind, ahead, along_z)
    full_found = [[first, second], [first_ahead, second_ahead],
                  [send(first_behind, along_s(1)), send(second_ahead, along_s(-1))], [first_behind, second_behind]]
    half_found = [half_z[d] for d in range(NZ)]

    codes = jnp.stack([kept_codes, received_codes])
    rows, cols = codes // 32, codes % 32

    group = jnp.arange(groups)[None, :, None] * NC
    pair, kind = rows // 3, rows % 3
    source_x = (group // (NC * NY)) * 2 + (2 * pair) // NZ
    source_y = (group // NC) % NY
    ahead_x, ahead_y = (source_x - x) % NX, (source_y - y) % NY
    ahead_s = jnp.where(core == 0, ahead_x, ahead_y)
    ahead_q = jnp.where(core == 0, ahead_y, ahead_x)
    first_z, second_z = (2 * pair - z) % NZ, (2 * pair + 1 - z) % NZ
    full_unit = ((ahead_s * 4 + ahead_q) * NZ + (2 * pair + kind // 2) % NZ) * 2
    half_unit = 256 + ahead_q * 4 + ahead_s
    split = kind == 1
    unit0 = jnp.where(split, half_unit + first_z * 16, full_unit).reshape(-1).astype(jnp.int32)
    unit1 = jnp.where(split, half_unit + second_z * 16, full_unit + 1).reshape(-1).astype(jnp.int32)
    columns = (cols + jnp.arange(2)[:, None, None] * 24).reshape(-1).astype(jnp.int32)
    last = jnp.max(jnp.where(codes != 0, jnp.arange(slots) + 1, 0), axis=2)
    counts = jnp.minimum(last + 1, slots).reshape(-1).astype(jnp.int32)

    chunks, places, at = [], [], 0
    for part in (piece for found in full_found for piece in found):
        chunks.append(part.reshape(-1, 64, width))
        places.append((at, chunks[-1].shape[0]))
        at += chunks[-1].shape[0]
    feature_pieces, feature_places = [], []
    for found in half_found:
        left = 16
        for piece in found:
            count = min(left, piece.shape[0])
            chunks.append(piece)
            places.append((at, count))
            at, left = at + count, left - count
            last_piece, last_count = piece, count
        feature_pieces.append(last_piece)
        feature_places.append(last_count)

    here = jnp.stack([core, own_rep // NZ, z]).astype(jnp.int32)
    own, other = products(by_parity, received, chunks, places, counts, unit0, unit1, columns, here)
    other, turned = together(send(other, flip), turn_features(feature_pieces, feature_places))
    partial = (own + other.astype(jnp.float32)).astype(jnp.bfloat16).reshape(2, NZ, -1, width)
    local_weight = features_product(partial, turned, here)
    near = lax.dynamic_index_in_dim(partial, own_rep // NZ, 0, keepdims=False)
    across = send(lax.dynamic_index_in_dim(partial, 1 - own_rep // NZ, 0, keepdims=False), across_x())
    own_rows = lax.all_to_all(local_weight, "rep", 0, 0, tiled=True).reshape(16, 16, width).sum(axis=0)
    line = (near.astype(jnp.float32) + across.astype(jnp.float32)).astype(jnp.bfloat16)
    line, own_rows = together(line, own_rows)
    terms = lax.all_to_all(line, BOTH, 0, 0, axis_index_groups=z_lines(), tiled=True)
    for partner in (other_core(), opposite_x(), paired_y(1), paired_y(2)):
        own_rows = own_rows + send(own_rows, partner)
    spread = jnp.broadcast_to(own_rows[None], (16, 16, width)).reshape(256, width)
    spread, terms = together(spread, terms)
    weight_grad = lax.all_to_all(spread, "rep", 0, 0, tiled=True)
    summed = terms.astype(jnp.float32).sum(axis=0)

    propagated = (inverse_root[:, None] * summed).astype(jnp.bfloat16)
    input_grad = lax.dot_general(
        propagated, weight, (((1,), (1,)), ((), ())), preferred_element_type=jnp.float32
    ).astype(jnp.bfloat16)
    return (input_grad, weight_grad)


def solution(mesh):
    placed = (
        P(("blk", "rep"), None),
        P(("blk", "rep"), None),
        P(("blk", "rep"), None),
        P(),
        P(("blk", "rep")),
        P(("blk", "rep"), None, None, None),
        P(("blk", "rep"), None),
        P(("blk", "rep"), None),
    )
    return jax.shard_map(
        body, mesh=mesh, in_specs=placed, out_specs=(P(("blk", "rep"), None), P()), check_vma=False
    )
```

```python
import jax
import jax.numpy as jnp
from jax import lax
from jax.experimental import pallas as pl
from jax.experimental.pallas import tpu as pltpu
from jax.sharding import PartitionSpec as P

NX, NY, NZ, NC = 4, 4, 8, 2
BOTH = ("blk", "rep")
UNROLL = 8


def flat_index(x, y, z, core):
    return (((x // 2) * NY + y) * NC + core) * (2 * NZ) + (x % 2) * NZ + z


def pairs(move):
    result = []
    for x in range(NX):
        for y in range(NY):
            for z in range(NZ):
                for core in range(NC):
                    tx, ty, tz, tc = move(x, y, z, core)
                    result.append((flat_index(x, y, z, core), flat_index(tx % NX, ty % NY, tz % NZ, tc)))
    return result


def along_z(step):
    return pairs(lambda x, y, z, core: (x, y, z + step, core))


def along_q(step):
    return pairs(lambda x, y, z, core: (x + step * core, y + step * (1 - core), z, core))


def along_s(step):
    return pairs(lambda x, y, z, core: (x + step * (1 - core), y + step * core, z, core))


def spread_over(value, places):
    count = len(places[0])
    copies = jnp.broadcast_to(value[None], (count, *value.shape))
    return lax.all_to_all(copies, BOTH, 0, 0, axis_index_groups=places, tiled=True)


def z_lines():
    return [[flat_index(x, y, z, c) for z in range(NZ)] for x in range(NX) for y in range(NY) for c in range(NC)]


def opposite_x():
    return pairs(lambda x, y, z, core: (x + 2, y, z, core))


def paired_y(bit):
    return pairs(lambda x, y, z, core: (x, y ^ bit, z, core))


def across_x():
    return pairs(lambda x, y, z, core: (x + 1 - 2 * (x % 2), y, z, core))


def other_core():
    return pairs(lambda x, y, z, core: (x, y, z, 1 - core))


def send(value, moves):
    return lax.ppermute(value, BOTH, moves)


def ring_first(value, along):
    return send(value, along(1)), send(value, along(-1))


def ring_last(behind, ahead, along):
    half = behind.shape[0] // 2
    return [send(behind[:half], along(1)), send(ahead[half:], along(-1))]


def together(*values):
    return lax.optimization_barrier(values)


def stacked(found):
    return jnp.stack([part[0] if len(part) == 1 else jnp.concatenate(part, axis=0) for part in found])


def products_kernel(places, counts, unit0, unit1, columns, here, kept, received, *rest):
    chunks = rest[: len(places)]
    own_out, other_out, units, totals, sem = rest[len(places):]
    step = pl.program_id(0)

    @pl.when(step == 0)
    def _():
        copies = [
            pltpu.make_async_copy(chunk.at[pl.ds(0, size)], units.at[pl.ds(start, size)], sem.at[n])
            for n, (chunk, (start, size)) in enumerate(zip(chunks, places))
        ]
        for copy in copies:
            copy.start()
        totals[...] = jnp.zeros_like(totals)
        for copy in copies:
            copy.wait()

    slots = kept.shape[2]
    starts = [(side * pl.num_programs(0) + step) * slots for side in range(2)]

    def batch(i, _):
        found = []
        for side, base in enumerate(starts):
            for k in range(UNROLL):
                slot = i * UNROLL + k
                entry = base + slot
                tile = received[0, slot] if side else kept[0, 0, slot]
                rows = jnp.concatenate([units[unit0[entry]], units[unit1[entry]]], axis=0)
                found.append((columns[entry], lax.dot_general(
                    tile, rows, (((0,), (0,)), ((), ())), preferred_element_type=jnp.float32)))
        for column, product in found:
            totals[column] += product
        return 0

    live = jnp.maximum(counts[step], counts[pl.num_programs(0) + step])
    lax.fori_loop(0, (live + UNROLL - 1) // UNROLL, batch, 0)

    @pl.when(step == pl.num_programs(0) - 1)
    def _():
        half = own_out.shape[0]
        own_out[...] = totals[:half]
        other_out[...] = totals[half:].astype(other_out.dtype)


def turn_kernel(places, *rest):
    pieces = rest[: len(places)]
    turned, held, sem = rest[len(places):]
    copies = [
        pltpu.make_async_copy(piece.at[pl.ds(start, held.shape[1])], held.at[n], sem.at[n])
        for n, (piece, start) in enumerate(zip(pieces, places))
    ]
    for copy in copies:
        copy.start()
    for n, copy in enumerate(copies):
        copy.wait()
        turned[n] = jnp.concatenate([held[n, k] for k in range(held.shape[1])], axis=0).T


def turn_features(pieces, places):
    width = pieces[0].shape[-1]
    return pl.pallas_call(
        lambda *refs: turn_kernel(places, *refs),
        out_shape=jax.ShapeDtypeStruct((NZ, width, 384), jnp.bfloat16),
        grid_spec=pltpu.PrefetchScalarGridSpec(
            num_scalar_prefetch=0,
            grid=(),
            in_specs=[pl.BlockSpec(memory_space=pl.ANY)] * NZ,
            out_specs=pl.BlockSpec(memory_space=pltpu.VMEM),
            scratch_shapes=[pltpu.VMEM((NZ, 6, 64, width), jnp.bfloat16), pltpu.SemaphoreType.DMA((NZ,))],
        ),
        compiler_params=pltpu.CompilerParams(vmem_limit_bytes=56 << 20),
        cost_estimate=pl.CostEstimate(flops=0, bytes_accessed=4 << 20, transcendentals=0),
        name="turn_features",
    )(*pieces)


def features_kernel(here, turned, partial, gradient):
    total = jnp.zeros(gradient.shape, jnp.float32)
    for place in range(NZ):
        ahead = lax.rem(place - here[2] + NZ, NZ)
        rows = jnp.concatenate([partial[here[1], place], partial[1 - here[1], place]], axis=0)
        total += jnp.dot(turned[ahead], rows, preferred_element_type=jnp.float32)
    gradient[...] = total


def features_product(partial, turned, here):
    width = partial.shape[-1]
    return pl.pallas_call(
        features_kernel,
        out_shape=jax.ShapeDtypeStruct((width, width), jnp.float32),
        grid_spec=pltpu.PrefetchScalarGridSpec(
            num_scalar_prefetch=1,
            grid=(),
            in_specs=[pl.BlockSpec(memory_space=pltpu.VMEM)] * 2,
            out_specs=pl.BlockSpec(memory_space=pltpu.VMEM),
        ),
        compiler_params=pltpu.CompilerParams(vmem_limit_bytes=24 << 20),
        cost_estimate=pl.CostEstimate(flops=2 * 3072 * width * width, bytes_accessed=4 << 20, transcendentals=0),
        name="features_product",
    )(here, turned, partial)


def pick_kernel(side, tiles, picked, held, in_sem, out_sem):
    groups = range(picked.shape[0])
    reads = [pltpu.make_async_copy(tiles.at[g, side[0]], held.at[g], in_sem.at[g]) for g in groups]
    writes = [pltpu.make_async_copy(held.at[g], picked.at[g], out_sem.at[g]) for g in groups]
    for read in reads:
        read.start()
    for read, write in zip(reads, writes):
        read.wait()
        write.start()
    for write in writes:
        write.wait()


def pick(tiles, side):
    groups, _, slots, block, _ = tiles.shape
    return pl.pallas_call(
        pick_kernel,
        out_shape=jax.ShapeDtypeStruct((groups, slots, block, block), tiles.dtype),
        grid_spec=pltpu.PrefetchScalarGridSpec(
            num_scalar_prefetch=1,
            grid=(),
            in_specs=[pl.BlockSpec(memory_space=pl.ANY)],
            out_specs=pl.BlockSpec(memory_space=pl.ANY),
            scratch_shapes=[
                pltpu.VMEM((groups, slots, block, block), tiles.dtype),
                pltpu.SemaphoreType.DMA((groups,)),
                pltpu.SemaphoreType.DMA((groups,)),
            ],
        ),
        compiler_params=pltpu.CompilerParams(vmem_limit_bytes=56 << 20),
        cost_estimate=pl.CostEstimate(flops=0, bytes_accessed=12 << 20, transcendentals=0),
        name="pick_tiles",
    )(side.reshape(1).astype(jnp.int32), tiles)


def products(tiles, received, chunks, places, counts, unit0, unit1, columns, here):
    groups, _, slots, block, _ = tiles.shape
    width = chunks[0].shape[-1]
    return pl.pallas_call(
        lambda *refs: products_kernel(places, *refs),
        out_shape=(
            jax.ShapeDtypeStruct((24, block, width), jnp.float32),
            jax.ShapeDtypeStruct((24, block, width), jnp.bfloat16),
        ),
        grid_spec=pltpu.PrefetchScalarGridSpec(
            num_scalar_prefetch=5,
            grid=(groups,),
            in_specs=[
                pl.BlockSpec((1, 1, slots, block, block), lambda g, n, u, v, k, here: (g, here[0], 0, 0, 0)),
                pl.BlockSpec((1, slots, block, block), lambda g, *_: (g, 0, 0, 0)),
            ] + [pl.BlockSpec(memory_space=pl.ANY)] * len(chunks),
            out_specs=(pl.BlockSpec((24, block, width), lambda g, *_: (0, 0, 0)),) * 2,
            scratch_shapes=[
                pltpu.VMEM((384, 64, width), jnp.bfloat16),
                pltpu.VMEM((48, block, width), jnp.float32),
                pltpu.SemaphoreType.DMA((len(chunks),)),
            ],
        ),
        compiler_params=pltpu.CompilerParams(vmem_limit_bytes=56 << 20),
        cost_estimate=pl.CostEstimate(flops=384 * 2 * block * block * width, bytes_accessed=30 << 20, transcendentals=0),
        name="tile_products",
    )(counts, unit0, unit1, columns, here, tiles, received, *chunks)


def body(out_grad, pre_act, features, weight, degrees, tiles, tile_rows, tile_cols):
    own_blk, own_rep = lax.axis_index("blk"), lax.axis_index("rep")
    core, y = own_blk % NC, (own_blk // NC) % NY
    x = (own_blk // (NC * NY)) * 2 + own_rep // NZ
    z = own_rep % NZ
    width = out_grad.shape[1]
    slots, block = tiles.shape[1], tiles.shape[2]
    groups = tiles.shape[0] // NC

    inverse_root = lax.rsqrt(degrees.astype(jnp.float32))
    active = (pre_act > 0).astype(jnp.float32)
    scaled = (out_grad.astype(jnp.float32) * active * inverse_root[:, None]).astype(jnp.bfloat16)

    rooted_features = (features.astype(jnp.float32) * inverse_root[:, None]).astype(jnp.bfloat16)

    odd = own_rep % 2
    full = lax.dynamic_slice_in_dim(scaled, odd * 64, 128, 0)
    half = lax.dynamic_slice_in_dim(scaled, (1 - odd) * 128, 64, 0)

    flip = other_core()
    by_parity = tiles.reshape(groups, NC, slots, block, block)
    codes = (tile_rows * 32 + tile_cols).reshape(groups, NC, slots)
    kept_codes = lax.dynamic_index_in_dim(codes, core, 1, keepdims=False)
    received_codes = send(lax.dynamic_index_in_dim(codes, 1 - core, 1, keepdims=False), flip)
    far_features = send(rooted_features, across_x())
    full_line = spread_over(full, z_lines())
    half_line = jnp.stack([half] + [send(half, along_s(-d)) for d in (1, 2, 3)])
    half_q = [half_line] + [send(half_line, along_q(-d)) for d in (1, 2, 3)]
    half_plane = jnp.concatenate(
        half_q + [rooted_features.reshape(-1, 64, width), far_features.reshape(-1, 64, width)])
    half_z = {0: [half_plane]}
    behind, ahead = ring_first(half_plane, along_z)
    q_behind, q_ahead = ring_first(full_line, along_q)
    q_behind, q_ahead, behind, ahead, side = together(q_behind, q_ahead, behind, ahead, 1 - core)
    picked = pick(by_parity, side)
    half_z[7], half_z[1] = [behind], [ahead]
    first = jnp.stack([full_line, q_ahead])
    q_opposite = send(q_behind, along_q(1))
    first_behind, first_ahead = ring_first(first, along_s)
    behind, ahead = send(behind, along_z(1)), send(ahead, along_z(-1))
    q_opposite, first_behind, first_ahead, behind, ahead, picked = together(
        q_opposite, first_behind, first_ahead, behind, ahead, picked)
    received = send(picked, flip)
    half_z[6], half_z[2] = [behind], [ahead]
    second = jnp.stack([q_opposite, q_behind])
    second_behind, second_ahead = ring_first(second, along_s)
    behind, ahead = send(behind, along_z(1)), send(ahead, along_z(-1))
    second_behind, second_ahead, behind, ahead, received = together(
        second_behind, second_ahead, behind, ahead, received)
    half_z[5], half_z[3] = [behind], [ahead]
    half_z[4] = ring_last(behind, ahead, along_z)
    full_found = [[first, second], [first_ahead, second_ahead],
                  [send(first_behind, along_s(1)), send(second_ahead, along_s(-1))], [first_behind, second_behind]]
    half_found = [half_z[d] for d in range(NZ)]

    codes = jnp.stack([kept_codes, received_codes])
    rows, cols = codes // 32, codes % 32

    group = jnp.arange(groups)[None, :, None] * NC
    pair, kind = rows // 3, rows % 3
    source_x = (group // (NC * NY)) * 2 + (2 * pair) // NZ
    source_y = (group // NC) % NY
    ahead_x, ahead_y = (source_x - x) % NX, (source_y - y) % NY
    ahead_s = jnp.where(core == 0, ahead_x, ahead_y)
    ahead_q = jnp.where(core == 0, ahead_y, ahead_x)
    first_z, second_z = (2 * pair - z) % NZ, (2 * pair + 1 - z) % NZ
    full_unit = ((ahead_s * 4 + ahead_q) * NZ + (2 * pair + kind // 2) % NZ) * 2
    half_unit = 256 + ahead_q * 4 + ahead_s
    split = kind == 1
    unit0 = jnp.where(split, half_unit + first_z * 16, full_unit).reshape(-1).astype(jnp.int32)
    unit1 = jnp.where(split, half_unit + second_z * 16, full_unit + 1).reshape(-1).astype(jnp.int32)
    columns = (cols + jnp.arange(2)[:, None, None] * 24).reshape(-1).astype(jnp.int32)
    last = jnp.max(jnp.where(codes != 0, jnp.arange(slots) + 1, 0), axis=2)
    counts = jnp.minimum(last + 1, slots).reshape(-1).astype(jnp.int32)

    chunks, places, at = [], [], 0
    for part in (piece for found in full_found for piece in found):
        chunks.append(part.reshape(-1, 64, width))
        places.append((at, chunks[-1].shape[0]))
        at += chunks[-1].shape[0]
    feature_pieces, feature_places = [], []
    for found in half_found:
        left = 16
        for piece in found:
            count = min(left, piece.shape[0])
            chunks.append(piece)
            places.append((at, count))
            at, left = at + count, left - count
            last_piece, last_count = piece, count
        feature_pieces.append(last_piece)
        feature_places.append(last_count)

    here = jnp.stack([core, own_rep // NZ, z]).astype(jnp.int32)
    own, other = products(by_parity, received, chunks, places, counts, unit0, unit1, columns, here)
    other, turned = together(send(other, flip), turn_features(feature_pieces, feature_places))
    partial = (own + other.astype(jnp.float32)).astype(jnp.bfloat16).reshape(2, NZ, -1, width)
    local_weight = features_product(partial, turned, here)
    near = lax.dynamic_index_in_dim(partial, own_rep // NZ, 0, keepdims=False)
    across = send(lax.dynamic_index_in_dim(partial, 1 - own_rep // NZ, 0, keepdims=False), across_x())
    own_rows = lax.all_to_all(local_weight, "rep", 0, 0, tiled=True).reshape(16, 16, width).sum(axis=0)
    line = (near.astype(jnp.float32) + across.astype(jnp.float32)).astype(jnp.bfloat16)
    line, own_rows = together(line, own_rows)
    terms = lax.all_to_all(line, BOTH, 0, 0, axis_index_groups=z_lines(), tiled=True)
    for partner in (other_core(), opposite_x(), paired_y(1), paired_y(2)):
        own_rows = own_rows + send(own_rows, partner)
    spread = jnp.broadcast_to(own_rows[None], (16, 16, width)).reshape(256, width)
    spread, terms = together(spread, terms)
    weight_grad = lax.all_to_all(spread, "rep", 0, 0, tiled=True)
    summed = terms.astype(jnp.float32).sum(axis=0)

    propagated = (inverse_root[:, None] * summed).astype(jnp.bfloat16)
    input_grad = lax.dot_general(
        propagated, weight, (((1,), (1,)), ((), ())), preferred_element_type=jnp.float32
    ).astype(jnp.bfloat16)
    return (input_grad, weight_grad)


def solution(mesh):
    placed = (
        P(("blk", "rep"), None),
        P(("blk", "rep"), None),
        P(("blk", "rep"), None),
        P(),
        P(("blk", "rep")),
        P(("blk", "rep"), None, None, None),
        P(("blk", "rep"), None),
        P(("blk", "rep"), None),
    )
    return jax.shard_map(
        body, mesh=mesh, in_specs=placed, out_specs=(P(("blk", "rep"), None), P()), check_vma=False
    )
```
